1024 devices in a mesh: row: 8 (over x, z_hi), col: 32 (over z_lo, core), pair: 4 (over y).
Axes of the slice: x: 4, y: 4, z: 32 (z_hi: 2, z_lo: 16; z = z_hi * 16 + z_lo), core: 2. Of those that a mesh axis runs over, the one named last changes fastest.
Arguments:
- factors: bfloat16 [1800, 512, 16], P('pair', ('row', 'col')), may hold values from -1 to 1
- amplitudes: bfloat16 [40, 16, 16], P('pair'), may hold values from -0.796875 to 0.796875
- virt_irreps: int32 [512], replicated, may hold values from 0 to 3
- win_irreps: int32 [16], replicated, may hold values from 0 to 3
- occ_irreps: int32 [120], replicated, may hold values from 0 to 3
- pair_list: int32 [40, 2], replicated, may hold values from 0 to 119
Outputs:
- ladder: float32 [40, 512, 8, 64], P('pair', 'row', None, 'col')
The draws below stay inside these ranges and needn't reach their ends.
All inputs are finite; a program needn't handle non-finite values.
Results may differ from the reference program's by a relative error of at most 0.0003.
Values may be sent and summed in bfloat16 or wider, within the bound.
A program may use at most 32 MiB of HBM per device.

```python
import jax
import jax.numpy as jnp
from jax import lax

NAUX = 1800
NV = 512
NOCC = 120
CW = 16
PAIRS = 40
N_ROW = 8


def set_ends(entries, stream_key, smallest, top_value):
    shape = entries.shape
    place = [jax.random.randint(jax.random.fold_in(stream_key, axis), (), 0, shape[axis]) for axis in range(len(shape))]
    entries = entries.at[tuple(place)].set(smallest)
    longest = shape.index(max(shape))
    place[longest] = (place[longest] + 1) % shape[longest]
    return entries.at[tuple(place)].set(top_value)


def levels(key, shape, cuts, least, top_value):
    def one(dim, shards_of):
        draws = jax.random.uniform(jax.random.fold_in(jax.random.fold_in(key, 6), dim), (shards_of,), jnp.float32, least / len(cuts), top_value / len(cuts))
        return jnp.repeat(jnp.exp(draws), shape[dim] // shards_of).reshape((-1,) + (1,) * (len(shape) - dim - 1))

    gain = one(*cuts[0])
    for cut in cuts[1:]:
        gain = gain * one(*cut)
    return gain


def gaussian(stream_key, dims, scale, reach, cuts=(), held_as=jnp.bfloat16):
    entries = scale * jax.random.normal(stream_key, dims, jnp.float32)
    if cuts:
        entries = entries * levels(stream_key, dims, cuts, -0.22, 0.18)
    return jnp.clip(entries, -reach, reach).astype(held_as)


def setup_inputs(seed: int = 0) -> dict:
    splits = jax.random.split(jax.random.key(seed), 7)
    factors = gaussian(splits[0], (NAUX, NV, CW), 0.15, 1.0, ((0, 4), (1, 256)))
    amplitudes = gaussian(splits[1], (PAIRS, CW, CW), 0.125, 0.796875, ((0, 4),))
    virt_irreps = set_ends(jax.random.randint(splits[2], (NV,), 0, 4), jax.random.fold_in(splits[2], 1), 0, 3).astype(jnp.int32)
    win_irreps = set_ends(jax.random.randint(splits[3], (CW,), 0, 4), jax.random.fold_in(splits[3], 1), 0, 3).astype(jnp.int32)
    occ_irreps = set_ends(jax.random.randint(splits[4], (NOCC,), 0, 4), jax.random.fold_in(splits[4], 1), 0, 3).astype(jnp.int32)
    pair_list = set_ends(jax.random.randint(splits[5], (PAIRS, 2), 0, NOCC), jax.random.fold_in(splits[5], 1), 0, NOCC - 1).astype(jnp.int32)
    return dict(factors=factors, amplitudes=amplitudes, virt_irreps=virt_irreps, win_irreps=win_irreps, occ_irreps=occ_irreps, pair_list=pair_list)


def reference(factors, amplitudes, virt_irreps, win_irreps, occ_irreps, pair_list):
    first = occ_irreps[pair_list[:, 0]]
    second = occ_irreps[pair_list[:, 1]]
    symmetry = jnp.bitwise_xor(first, second)
    product = jnp.bitwise_xor(win_irreps[:, None], win_irreps[None, :])
    weights = jnp.where(product[None, :, :] == symmetry[:, None, None], amplitudes.astype(jnp.float32), 0.0)
    block_rows = min(64, NV)
    columns = factors.reshape(NAUX, NV * CW)

    def one_block(index):
        rows = lax.dynamic_slice_in_dim(factors, index * block_rows, block_rows, 1).reshape(NAUX, block_rows * CW)
        integral = lax.dot_general(rows, columns, (((0,), (0,)), ((), ())), preferred_element_type=jnp.float32)
        integral = integral.reshape(block_rows, CW, NV, CW)
        return jnp.einsum("acbd,pcd->pab", integral.astype(jnp.float32), weights, precision=lax.Precision.HIGHEST)

    blocks = lax.map(one_block, jnp.arange(NV // block_rows, dtype=jnp.int32))
    full = jnp.transpose(blocks, (1, 0, 2, 3)).reshape(PAIRS, NV, NV)
    pair_sym = jnp.bitwise_xor(virt_irreps[:, None], virt_irreps[None, :])
    result = jnp.where(pair_sym[None, :, :] == symmetry[:, None, None], full, 0.0)
    return result.reshape(PAIRS, NV, N_ROW, NV // N_ROW)
```

```python
import jax
import jax.numpy as jnp
from jax import lax
from jax.sharding import PartitionSpec as P


def lookup_symmetry(occ_irreps, pair_list):
    labels = jnp.arange(occ_irreps.shape[0], dtype=jnp.int32)
    onehot = pair_list[:, :, None] == labels[None, None, :]
    picked = jnp.sum(jnp.where(onehot, occ_irreps[None, None, :], 0), axis=-1)
    return jnp.bitwise_xor(picked[:, 0], picked[:, 1])


def mask_amplitudes(amplitudes, win_irreps, symmetry):
    product = jnp.bitwise_xor(win_irreps[:, None], win_irreps[None, :])
    allowed = product[None, :, :] == symmetry[:, None, None]
    return jnp.where(allowed, amplitudes.astype(jnp.float32), 0.0)


def body(factors, amplitudes, virt_irreps, win_irreps, occ_irreps, pair_list):
    per_device = factors.shape[1]
    n_rows = lax.axis_size("row")
    n_cols = lax.axis_size("col")
    block_a = per_device * n_cols
    slab = amplitudes.shape[0]
    symmetry_all = lookup_symmetry(occ_irreps, pair_list)
    own_symmetry = lax.dynamic_slice_in_dim(symmetry_all, lax.axis_index("pair") * slab, slab)
    all_amplitudes = lax.all_gather(amplitudes, "pair", axis=0, tiled=True)
    weights = mask_amplitudes(all_amplitudes, win_irreps, symmetry_all)
    n_fitting = factors.shape[0]
    width = factors.shape[2]
    b_rows = lax.all_gather(factors, "row", axis=1, tiled=True)
    b_matrix = b_rows.reshape(n_fitting, n_rows * per_device * width)
    panel_rows = lax.all_gather(factors, "col", axis=1, tiled=True)
    count = panel_rows.shape[1]
    integral = lax.dot_general(
        panel_rows.reshape(n_fitting, count * width),
        b_matrix,
        (((0,), (0,)), ((), ())),
        preferred_element_type=jnp.float32,
    )
    integral = integral.reshape(count, width, n_rows * per_device, width)
    partial = jnp.einsum("acbd,pcd->pab", integral, weights, precision=lax.Precision.HIGHEST)
    total = lax.psum_scatter(partial, "pair", scatter_dimension=0, tiled=True)
    total = total.reshape(slab, count, n_rows, per_device)
    a_labels = lax.dynamic_slice_in_dim(virt_irreps, lax.axis_index("row") * block_a, block_a)
    b_labels = lax.dynamic_slice_in_dim(
        virt_irreps.reshape(n_rows, -1), lax.axis_index("col") * per_device, per_device, 1
    )
    pair_sym = jnp.bitwise_xor(a_labels[:, None, None], b_labels[None, :, :])
    allowed = pair_sym[None, :, :, :] == own_symmetry[:, None, None, None]
    return jnp.where(allowed, total, 0.0)


def solution(mesh):
    in_specs = (P("pair", ("row", "col"), None), P("pair", None, None), P(), P(), P(), P())
    out_specs = P("pair", "row", None, "col")
    return jax.shard_map(body, mesh=mesh, in_specs=in_specs, out_specs=out_specs, check_vma=False)
```

```python
import functools

import jax
import jax.numpy as jnp
from jax import lax
from jax.experimental import pallas as pl
from jax.experimental.pallas import tpu as pltpu
from jax.sharding import PartitionSpec as P

MESH = pl.DeviceIdType.MESH
LANES = 512
GROUP = 4


def kernel(
    dims, x_ref, amp_ref, virt_ref, win_ref, occ_ref, pairs_ref, out_ref,
    a_buf, b_buf, w_buf, wide, integral, parts, sums, inbox,
    a_send, a_recv, b_send, b_recv, w_send, w_recv, r_send, r_recv,
):
    n_rows, n_cols, n_pairs, slab = dims
    row, col, pair = lax.axis_index("row"), lax.axis_index("col"), lax.axis_index("pair")
    width = amp_ref.shape[2]
    height = 2 * width
    n_fit = x_ref.shape[2]
    n_groups = n_cols // 2 // GROUP
    n_x = n_rows // 2
    core = lax.rem(col, 2)
    place = lax.rem(lax.div(col, 2), GROUP)
    group = lax.div(lax.div(col, 2), GROUP)

    def column(g, p):
        return (g * GROUP + p) * 2 + core

    def at(r=None, c=None, p=None):
        return (row if r is None else r, col if c is None else c, pair if p is None else p)

    far = [column(jnp.bitwise_xor(group, k), place) for k in range(1, n_groups)]
    near = [column(group, jnp.bitwise_xor(place, j)) for j in range(1, GROUP)]
    mate = jnp.bitwise_xor(col, 1)
    partner = jnp.bitwise_xor(row, 1)
    sides = [jnp.bitwise_xor(row, 2 * k) for k in range(1, n_x)]
    others = [jnp.bitwise_xor(pair, k) for k in range(1, n_pairs)]

    peers = [at(c=c) for c in far + near + [mate]]
    peers += [at(r=r) for r in [partner] + sides] + [at(p=p) for p in others]
    barrier = pltpu.get_barrier_semaphore()
    for peer in peers:
        pl.semaphore_signal(barrier, inc=1, device_id=peer, device_id_type=MESH)

    own = jnp.concatenate([x_ref[0], x_ref[1]], axis=0)
    own = jnp.concatenate([own, jnp.zeros((height, LANES - n_fit), own.dtype)], axis=1)
    a_buf[col] = own
    b_buf[row] = own

    symmetry = []
    for s in range(slab):
        first, second = pairs_ref[0, pair * slab + s], pairs_ref[1, pair * slab + s]
        symmetry.append(jnp.bitwise_xor(occ_ref[first], occ_ref[second]))
    down = lax.broadcasted_iota(jnp.int32, (width, width), 0)
    across = lax.broadcasted_iota(jnp.int32, (width, width), 1)
    product = jnp.zeros((width, width), jnp.int32)
    for j in range(width):
        label = win_ref[j]
        product = jnp.bitwise_xor(product, jnp.where(down == j, label, 0))
        product = jnp.bitwise_xor(product, jnp.where(across == j, label, 0))
    for s in range(slab):
        kept = jnp.where(product == symmetry[s], amp_ref[s].astype(jnp.float32), 0.0)
        w_buf[pair, s * width:(s + 1) * width, :] = kept.astype(jnp.bfloat16)

    pl.semaphore_wait(barrier, len(peers))
    started = []

    def send(src, dst, sems, slot, recv, target):
        copy = pltpu.make_async_remote_copy(
            src_ref=src, dst_ref=dst, send_sem=sems.at[slot], recv_sem=recv, device_id=target, device_id_type=MESH
        )
        copy.start()
        started.append(copy)

    counts = {"a": 0, "b": 0}

    def send_a(slot, c):
        send(a_buf.at[slot], a_buf.at[slot], a_send, counts["a"], a_recv.at[slot], at(c=c))
        counts["a"] += 1

    def send_b(slot, r):
        send(b_buf.at[slot], b_buf.at[slot], b_send, counts["b"], b_recv.at[slot], at(r=r))
        counts["b"] += 1

    def arrived(buf, recv, sems, slot, peer):
        pltpu.make_async_remote_copy(
            src_ref=buf.at[slot], dst_ref=buf.at[slot], send_sem=sems.at[0], recv_sem=recv.at[slot],
            device_id=peer, device_id_type=MESH,
        ).wait_recv()

    send_b(row, partner)
    for c in reversed(far):
        send_a(col, c)
    for c in near:
        send_a(col, c)
    for i, p in enumerate(others):
        send(w_buf.at[pair], w_buf.at[pair], w_send, i, w_recv.at[pair], at(p=p))
    for r in sides:
        send_b(row, r)
    send_a(col, mate)

    def relay(slot, source):
        arrived(a_buf, a_recv, a_send, slot, at(c=source))
        for c in near:
            send_a(slot, c)
        send_a(slot, mate)

    def handover(slot, source):
        arrived(a_buf, a_recv, a_send, slot, at(c=source))
        send_a(slot, mate)

    span = n_rows * 2 * width
    spread = (
        lax.rem(lax.broadcasted_iota(jnp.int32, (width, span), 1), width)
        == lax.broadcasted_iota(jnp.int32, (width, span), 0)
    ).astype(jnp.bfloat16)
    own_b = (
        lax.div(lax.broadcasted_iota(jnp.int32, (n_rows * 2, span), 1), width)
        == lax.broadcasted_iota(jnp.int32, (n_rows * 2, span), 0)
    )

    def expand(p):
        def one(s, carry):
            lines = jnp.dot(
                w_buf[p, pl.ds(pl.multiple_of(s * width, width), width), :], spread, preferred_element_type=jnp.float32
            )
            start = pl.multiple_of((p * slab + s) * n_rows * 2, n_rows * 2)
            for c in range(width):
                block = jnp.where(own_b, jnp.broadcast_to(lines[c:c + 1, :], own_b.shape), 0.0)
                wide[pl.ds(start, n_rows * 2), c * span:(c + 1) * span] = block.astype(jnp.bfloat16)
            return carry

        lax.fori_loop(0, slab, one, 0)

    expand(pair)
    relay(far[0], far[0])
    for j, c in enumerate(near):
        handover(c, c)
    for p in others[:1]:
        arrived(w_buf, w_recv, w_send, p, at(p=p))
        expand(p)
    relay(far[1], far[1])
    for p in others[1:]:
        arrived(w_buf, w_recv, w_send, p, at(p=p))
        expand(p)
    relay(far[2], far[2])
    for j in range(1, GROUP):
        slot = column(jnp.bitwise_xor(group, 1), jnp.bitwise_xor(place, j))
        handover(slot, near[j - 1])
    arrived(b_buf, b_recv, b_send, partner, at(r=partner))
    for r in sides:
        send_b(partner, r)
    for k in range(2, n_groups):
        for j in range(1, GROUP):
            slot = column(jnp.bitwise_xor(group, k), jnp.bitwise_xor(place, j))
            handover(slot, near[j - 1])
    for r in sides:
        arrived(b_buf, b_recv, b_send, r, at(r=r))
        arrived(b_buf, b_recv, b_send, jnp.bitwise_xor(r, 1), at(r=r))
    for c in range(n_cols // 2):
        slot = 2 * c + 1 - core
        arrived(a_buf, a_recv, a_send, slot, at(c=mate))

    n_a = 2 * n_cols
    b_all = b_buf[...].reshape(span, LANES)
    chunk = 8

    def multiply(i, carry):
        first = pl.multiple_of(i * chunk, chunk)
        rows = a_buf[pl.ds(first, chunk)].reshape(chunk * height, LANES)
        tile = lax.dot_general(rows, b_all, (((1,), (1,)), ((), ())), preferred_element_type=jnp.float32)
        for t in range(span // 128):
            integral[t, pl.ds(pl.multiple_of(first * height, chunk * height), chunk * height), :] = (
                tile[:, t * 128:(t + 1) * 128]
            )
        return carry

    lax.fori_loop(0, n_cols // chunk, multiply, 0)
    for c in range(width):
        for t in range(span // 128):
            lines = integral[t, pl.ds(c, n_a, stride=width), :]
            high = lines.astype(jnp.bfloat16)
            first = c * span + t * 128
            parts[0:n_a, first:first + 128] = high
            parts[n_a:2 * n_a, first:first + 128] = (lines - high.astype(jnp.float32)).astype(jnp.bfloat16)

    tall = slab * n_rows * 2
    half = tall // 2

    def residual(p):
        start = pl.multiple_of(p * tall, tall)
        both = lax.dot_general(
            wide[pl.ds(start, tall), :], parts[...], (((1,), (1,)), ((), ())), preferred_element_type=jnp.float32
        )
        whole = both[:, 0:n_a] + both[:, n_a:2 * n_a]
        return jnp.concatenate([whole[0:half], whole[half:tall]], axis=1)

    for i, p in enumerate(others):
        sums[p] = residual(p)
        send(sums.at[p], inbox.at[pair], r_send, i, r_recv.at[pair], at(p=p))
    total = residual(pair)

    lane = lax.broadcasted_iota(jnp.int32, (n_rows * 2, 2 * n_a), 1)
    line = lax.broadcasted_iota(jnp.int32, (n_rows * 2, 2 * n_a), 0)
    label = jnp.zeros((n_rows * 2, 2 * n_a), jnp.int32)
    lane_a = lax.rem(lane, n_a)
    for j in range(n_a):
        label = jnp.where(lane_a == j, virt_ref[row * n_a + j], label)
    for k in range(n_rows):
        for m in range(2):
            label = jnp.bitwise_xor(label, jnp.where(line == 2 * k + m, virt_ref[k * n_a + col * 2 + m], 0))

    for p in others:
        arrived(inbox, r_recv, r_send, p, at(p=p))
        total = total + inbox[p]
    deep = n_rows * 2
    for s in range(slab // 2):
        wanted = jnp.where(lane < n_a, symmetry[s], symmetry[s + slab // 2])
        kept = jnp.where(label == wanted, total[s * deep:(s + 1) * deep], 0.0)
        out_ref[s] = kept[:, 0:n_a]
        out_ref[s + slab // 2] = kept[:, n_a:2 * n_a]
    for copy in started:
        copy.wait_send()


def body(factors, amplitudes, virt_irreps, win_irreps, occ_irreps, pair_list):
    n_rows, n_cols, n_pairs = (lax.axis_size(name) for name in ("row", "col", "pair"))
    slab, width = amplitudes.shape[0], amplitudes.shape[1]
    per_device = factors.shape[1]
    n_a = per_device * n_cols
    span = n_rows * per_device * width
    n_b = n_rows * per_device
    n_groups = n_cols // 2 // GROUP
    n_x = n_rows // 2
    height = per_device * width
    a_sends = (n_groups - 1) + n_groups * (GROUP - 1) + n_cols // 2
    b_sends = 1 + 2 * (n_x - 1)
    vmem, smem = pl.BlockSpec(memory_space=pltpu.VMEM), pl.BlockSpec(memory_space=pltpu.SMEM)
    dma = pltpu.SemaphoreType.DMA
    out = pl.pallas_call(
        functools.partial(kernel, (n_rows, n_cols, n_pairs, slab)),
        out_shape=jax.ShapeDtypeStruct((slab, n_b, n_a), jnp.float32),
        in_specs=[vmem, vmem, smem, smem, smem, smem],
        out_specs=vmem,
        scratch_shapes=[
            pltpu.VMEM((n_cols, height, LANES), jnp.bfloat16),
            pltpu.VMEM((n_rows, height, LANES), jnp.bfloat16),
            pltpu.VMEM((n_pairs, slab * width, width), jnp.bfloat16),
            pltpu.VMEM((n_pairs * slab * n_b, width * span), jnp.bfloat16),
            pltpu.VMEM((span // 128, n_a * width, 128), jnp.float32),
            pltpu.VMEM((2 * n_a, width * span), jnp.bfloat16),
            pltpu.VMEM((n_pairs, slab * n_b // 2, 2 * n_a), jnp.float32),
            pltpu.VMEM((n_pairs, slab * n_b // 2, 2 * n_a), jnp.float32),
            dma((a_sends,)), dma((n_cols,)),
            dma((b_sends,)), dma((n_rows,)),
            dma((n_pairs,)), dma((n_pairs,)),
            dma((n_pairs,)), dma((n_pairs,)),
        ],
        compiler_params=pltpu.CompilerParams(
            collective_id=0, has_side_effects=True, vmem_limit_bytes=32 * 1024 * 1024
        ),
        name="ladder",
    )(jnp.transpose(factors, (1, 2, 0)), amplitudes, virt_irreps, win_irreps, occ_irreps, pair_list.T)
    return jnp.transpose(out.reshape(slab, n_rows, per_device, n_a), (0, 3, 1, 2))


def solution(mesh):
    in_specs = (P("pair", ("row", "col"), None), P("pair", None, None), P(), P(), P(), P())
    out_specs = P("pair", "row", None, "col")
    return jax.shard_map(body, mesh=mesh, in_specs=in_specs, out_specs=out_specs, check_vma=False)
```

```python
import functools

import jax
import jax.numpy as jnp
from jax import lax
from jax.experimental import pallas as pl
from jax.experimental.pallas import tpu as pltpu
from jax.sharding import PartitionSpec as P

MESH = pl.DeviceIdType.MESH
LANES = 512
GROUP = 4


def kernel(
    dims, x_hbm, amp_hbm, virt_hbm, win_hbm, occ_hbm, pairs_hbm, out_ref,
    x_ref, amp_ref, virt_ref, win_ref, occ_ref, pairs_ref, local,
    a_buf, b_buf, w_buf, wide, integral, parts, sums, inbox,
    a_send, a_recv, b_send, b_recv, w_send, w_recv, r_send, r_recv, f_send,
):
    n_rows, n_cols, n_pairs, slab = dims
    row, col, pair = lax.axis_index("row"), lax.axis_index("col"), lax.axis_index("pair")
    width = amp_ref.shape[2]
    height = 2 * width
    n_fit = x_ref.shape[2]
    n_groups = n_cols // 2 // GROUP
    n_x = n_rows // 2
    core = lax.rem(col, 2)
    place = lax.rem(lax.div(col, 2), GROUP)
    group = lax.div(lax.div(col, 2), GROUP)

    def column(g, p):
        return (g * GROUP + p) * 2 + core

    def at(r=None, c=None, p=None):
        return (row if r is None else r, col if c is None else c, pair if p is None else p)

    far = [column(jnp.bitwise_xor(group, k), place) for k in range(1, n_groups)]
    near = [column(group, jnp.bitwise_xor(place, j)) for j in range(1, GROUP)]
    mate = jnp.bitwise_xor(col, 1)
    partner = jnp.bitwise_xor(row, 1)
    sides = [jnp.bitwise_xor(row, 2 * k) for k in range(1, n_x)]
    others = [jnp.bitwise_xor(pair, k) for k in range(1, n_pairs)]

    higher = [jnp.bitwise_xor(group, k) > group for k in range(1, n_groups)]
    upper = jnp.bitwise_and(row, 1) == 1

    barrier = pltpu.get_barrier_semaphore()

    def greet(peer):
        pl.semaphore_signal(barrier, inc=1, device_id=peer, device_id_type=MESH)

    peers = [at(c=c) for c in near + [mate]] + [at(r=r) for r in sides] + [at(p=p) for p in others]
    for peer in peers:
        greet(peer)
    for c, up in zip(far, higher):
        pl.when(up)(functools.partial(greet, at(c=c)))
    pl.when(jnp.logical_not(upper))(functools.partial(greet, at(r=partner)))

    loads = []
    pairs_of = ((x_hbm, x_ref), (amp_hbm, amp_ref), (win_hbm, win_ref), (occ_hbm, occ_ref), (pairs_hbm, pairs_ref), (virt_hbm, virt_ref))
    for i, (src, dst) in enumerate(pairs_of):
        loads.append(pltpu.make_async_copy(src, dst, local.at[i]))
        loads[i].start()

    loads[0].wait()
    own = jnp.concatenate([x_ref[0], x_ref[1]], axis=0)
    own = jnp.concatenate([own, jnp.zeros((height, LANES - n_fit), own.dtype)], axis=1)
    a_buf[col] = own
    b_buf[row] = own

    pl.semaphore_wait(barrier, len(peers) + group + jnp.bitwise_and(row, 1))
    started = []

    def send(src, dst, sems, slot, recv, target):
        copy = pltpu.make_async_remote_copy(
            src_ref=src, dst_ref=dst, send_sem=sems.at[slot], recv_sem=recv, device_id=target, device_id_type=MESH
        )
        copy.start()
        started.append(copy)

    counts = {"a": 0, "b": 0}

    def send_a(slot, c):
        send(a_buf.at[slot], a_buf.at[slot], a_send, counts["a"], a_recv.at[slot], at(c=c))
        counts["a"] += 1

    def send_b(slot, r):
        send(b_buf.at[slot], b_buf.at[slot], b_send, counts["b"], b_recv.at[slot], at(r=r))
        counts["b"] += 1

    def arrived(buf, recv, sems, slot, peer):
        pltpu.make_async_remote_copy(
            src_ref=buf.at[slot], dst_ref=buf.at[slot], send_sem=sems.at[0], recv_sem=recv.at[slot],
            device_id=peer, device_id_type=MESH,
        ).wait_recv()

    def to_partner():
        pltpu.make_async_remote_copy(
            src_ref=b_buf.at[row], dst_ref=b_buf.at[row], send_sem=b_send.at[2 * len(sides)], recv_sem=b_recv.at[row],
            device_id=at(r=partner), device_id_type=MESH,
        ).start()

    def to_far(k):
        pltpu.make_async_remote_copy(
            src_ref=a_buf.at[col], dst_ref=a_buf.at[col], send_sem=f_send.at[k], recv_sem=a_recv.at[col],
            device_id=at(c=far[k]), device_id_type=MESH,
        ).start()

    pl.when(upper)(to_partner)
    for k in reversed(range(len(far))):
        pl.when(jnp.logical_not(higher[k]))(functools.partial(to_far, k))
    for c in near:
        send_a(col, c)
    for r in sides:
        send_b(row, r)
    send_a(col, mate)

    for load in loads[1:]:
        load.wait()
    symmetry = []
    for s in range(slab):
        first, second = pairs_ref[0, pair * slab + s], pairs_ref[1, pair * slab + s]
        symmetry.append(jnp.bitwise_xor(occ_ref[first], occ_ref[second]))
    down = lax.broadcasted_iota(jnp.int32, (width, width), 0)
    across = lax.broadcasted_iota(jnp.int32, (width, width), 1)
    product = jnp.zeros((width, width), jnp.int32)
    for j in range(width):
        label = win_ref[j]
        product = jnp.bitwise_xor(product, jnp.where(down == j, label, 0))
        product = jnp.bitwise_xor(product, jnp.where(across == j, label, 0))
    for s in range(slab):
        kept = jnp.where(product == symmetry[s], amp_ref[s].astype(jnp.float32), 0.0)
        w_buf[pair, s * width:(s + 1) * width, :] = kept.astype(jnp.bfloat16)
    for i, p in enumerate(others):
        send(w_buf.at[pair], w_buf.at[pair], w_send, i, w_recv.at[pair], at(p=p))

    def relay(k):
        slot = far[k]
        arrived(a_buf, a_recv, a_send, slot, at(c=slot))
        pl.when(higher[k])(functools.partial(to_far, k))
        for c in near:
            send_a(slot, c)
        send_a(slot, mate)

    def handover(slot, source):
        arrived(a_buf, a_recv, a_send, slot, at(c=source))
        send_a(slot, mate)

    span = n_rows * 2 * width
    spread = (
        lax.rem(lax.broadcasted_iota(jnp.int32, (width, span), 1), width)
        == lax.broadcasted_iota(jnp.int32, (width, span), 0)
    ).astype(jnp.bfloat16)
    own_b = (
        lax.div(lax.broadcasted_iota(jnp.int32, (n_rows * 2, span), 1), width)
        == lax.broadcasted_iota(jnp.int32, (n_rows * 2, span), 0)
    )

    def expand(p):
        def one(s, carry):
            lines = jnp.dot(
                w_buf[p, pl.ds(pl.multiple_of(s * width, width), width), :], spread, preferred_element_type=jnp.float32
            )
            start = pl.multiple_of((p * slab + s) * n_rows * 2, n_rows * 2)
            for c in range(width):
                block = jnp.where(own_b, jnp.broadcast_to(lines[c:c + 1, :], own_b.shape), 0.0)
                wide[pl.ds(start, n_rows * 2), c * span:(c + 1) * span] = block.astype(jnp.bfloat16)
            return carry

        lax.fori_loop(0, slab, one, 0)

    expand(pair)
    relay(0)
    for j, c in enumerate(near):
        handover(c, c)
    for p in others[:1]:
        arrived(w_buf, w_recv, w_send, p, at(p=p))
        expand(p)
    relay(1)
    for p in others[1:]:
        arrived(w_buf, w_recv, w_send, p, at(p=p))
        expand(p)
    relay(2)
    for j in range(1, GROUP):
        slot = column(jnp.bitwise_xor(group, 1), jnp.bitwise_xor(place, j))
        handover(slot, near[j - 1])
    def across_z():
        arrived(b_buf, b_recv, b_send, partner, at(r=partner))
        pl.when(jnp.logical_not(upper))(to_partner)
        for i, r in enumerate(sides):
            pltpu.make_async_remote_copy(
                src_ref=b_buf.at[partner], dst_ref=b_buf.at[partner], send_sem=b_send.at[len(sides) + i],
                recv_sem=b_recv.at[partner], device_id=at(r=r), device_id_type=MESH,
            ).start()

    pl.when(jnp.logical_not(upper))(across_z)
    for k in range(2, n_groups):
        for j in range(1, GROUP):
            slot = column(jnp.bitwise_xor(group, k), jnp.bitwise_xor(place, j))
            handover(slot, near[j - 1])
    pl.when(upper)(across_z)
    for r in sides:
        arrived(b_buf, b_recv, b_send, r, at(r=r))
        arrived(b_buf, b_recv, b_send, jnp.bitwise_xor(r, 1), at(r=r))
    for c in range(n_cols // 2):
        slot = 2 * c + 1 - core
        arrived(a_buf, a_recv, a_send, slot, at(c=mate))

    n_a = 2 * n_cols
    b_all = b_buf[...].reshape(span, LANES)
    chunk = 8

    def multiply(i, carry):
        first = pl.multiple_of(i * chunk, chunk)
        rows = a_buf[pl.ds(first, chunk)].reshape(chunk * height, LANES)
        tile = lax.dot_general(rows, b_all, (((1,), (1,)), ((), ())), preferred_element_type=jnp.float32)
        for t in range(span // 128):
            integral[t, pl.ds(pl.multiple_of(first * height, chunk * height), chunk * height), :] = (
                tile[:, t * 128:(t + 1) * 128]
            )
        return carry

    lax.fori_loop(0, n_cols // chunk, multiply, 0)
    for c in range(width):
        for t in range(span // 128):
            lines = integral[t, pl.ds(c, n_a, stride=width), :]
            high = lines.astype(jnp.bfloat16)
            first = c * span + t * 128
            parts[0:n_a, first:first + 128] = high
            parts[n_a:2 * n_a, first:first + 128] = (lines - high.astype(jnp.float32)).astype(jnp.bfloat16)

    tall = slab * n_rows * 2
    half = tall // 2

    def residual(p):
        start = pl.multiple_of(p * tall, tall)
        both = lax.dot_general(
            wide[pl.ds(start, tall), :], parts[...], (((1,), (1,)), ((), ())), preferred_element_type=jnp.float32
        )
        whole = both[:, 0:n_a] + both[:, n_a:2 * n_a]
        return jnp.concatenate([whole[0:half], whole[half:tall]], axis=1)

    for i, p in enumerate(others):
        sums[p] = residual(p)
        send(sums.at[p], inbox.at[pair], r_send, i, r_recv.at[pair], at(p=p))
    total = residual(pair)

    lane = lax.broadcasted_iota(jnp.int32, (n_rows * 2, 2 * n_a), 1)
    line = lax.broadcasted_iota(jnp.int32, (n_rows * 2, 2 * n_a), 0)
    label = jnp.zeros((n_rows * 2, 2 * n_a), jnp.int32)
    lane_a = lax.rem(lane, n_a)
    for j in range(n_a):
        label = jnp.where(lane_a == j, virt_ref[row * n_a + j], label)
    for k in range(n_rows):
        for m in range(2):
            label = jnp.bitwise_xor(label, jnp.where(line == 2 * k + m, virt_ref[k * n_a + col * 2 + m], 0))

    for p in others:
        arrived(inbox, r_recv, r_send, p, at(p=p))
        total = total + inbox[p]
    deep = n_rows * 2
    for s in range(slab // 2):
        wanted = jnp.where(lane < n_a, symmetry[s], symmetry[s + slab // 2])
        kept = jnp.where(label == wanted, total[s * deep:(s + 1) * deep], 0.0)
        out_ref[s] = kept[:, 0:n_a]
        out_ref[s + slab // 2] = kept[:, n_a:2 * n_a]
    for copy in started:
        copy.wait_send()

    def sent(buf, slot, sem, target):
        pltpu.make_async_remote_copy(
            src_ref=buf.at[slot], dst_ref=buf.at[slot], send_sem=sem, recv_sem=sem, device_id=target, device_id_type=MESH
        ).wait_send()

    for k, c in enumerate(far):
        sent(a_buf, col, f_send.at[k], at(c=c))
    for i, r in enumerate(sides):
        sent(b_buf, partner, b_send.at[len(sides) + i], at(r=r))
    sent(b_buf, row, b_send.at[2 * len(sides)], at(r=partner))


def body(factors, amplitudes, virt_irreps, win_irreps, occ_irreps, pair_list):
    n_rows, n_cols, n_pairs = (lax.axis_size(name) for name in ("row", "col", "pair"))
    slab, width = amplitudes.shape[0], amplitudes.shape[1]
    per_device = factors.shape[1]
    n_a = per_device * n_cols
    span = n_rows * per_device * width
    n_b = n_rows * per_device
    n_groups = n_cols // 2 // GROUP
    n_x = n_rows // 2
    height = per_device * width
    a_sends = n_groups * (GROUP - 1) + n_cols // 2
    b_sends = 1 + 2 * (n_x - 1)
    hbm = pl.BlockSpec(memory_space=pltpu.HBM)
    dma = pltpu.SemaphoreType.DMA
    out = pl.pallas_call(
        functools.partial(kernel, (n_rows, n_cols, n_pairs, slab)),
        out_shape=jax.ShapeDtypeStruct((slab, n_b, n_a), jnp.float32),
        in_specs=[hbm] * 6,
        out_specs=pl.BlockSpec(memory_space=pltpu.VMEM),
        scratch_shapes=[
            pltpu.VMEM((per_device, width, factors.shape[0]), factors.dtype),
            pltpu.VMEM(amplitudes.shape, amplitudes.dtype),
            pltpu.SMEM(virt_irreps.shape, jnp.int32),
            pltpu.SMEM(win_irreps.shape, jnp.int32),
            pltpu.SMEM(occ_irreps.shape, jnp.int32),
            pltpu.SMEM(pair_list.shape[::-1], jnp.int32),
            dma((6,)),
            pltpu.VMEM((n_cols, height, LANES), jnp.bfloat16),
            pltpu.VMEM((n_rows, height, LANES), jnp.bfloat16),
            pltpu.VMEM((n_pairs, slab * width, width), jnp.bfloat16),
            pltpu.VMEM((n_pairs * slab * n_b, width * span), jnp.bfloat16),
            pltpu.VMEM((span // 128, n_a * width, 128), jnp.float32),
            pltpu.VMEM((2 * n_a, width * span), jnp.bfloat16),
            pltpu.VMEM((n_pairs, slab * n_b // 2, 2 * n_a), jnp.float32),
            pltpu.VMEM((n_pairs, slab * n_b // 2, 2 * n_a), jnp.float32),
            dma((a_sends,)), dma((n_cols,)),
            dma((b_sends,)), dma((n_rows,)),
            dma((n_pairs,)), dma((n_pairs,)),
            dma((n_pairs,)), dma((n_pairs,)), dma((n_groups - 1,)),
        ],
        compiler_params=pltpu.CompilerParams(
            collective_id=0, has_side_effects=True, vmem_limit_bytes=56 * 1024 * 1024
        ),
        name="ladder",
    )(jnp.transpose(factors, (1, 2, 0)), amplitudes, virt_irreps, win_irreps, occ_irreps, pair_list.T)
    return jnp.transpose(out.reshape(slab, n_rows, per_device, n_a), (0, 3, 1, 2))


def solution(mesh):
    in_specs = (P("pair", ("row", "col"), None), P("pair", None, None), P(), P(), P(), P())
    out_specs = P("pair", "row", None, "col")
    return jax.shard_map(body, mesh=mesh, in_specs=in_specs, out_specs=out_specs, check_vma=False)
```

```python
import functools

import jax
import jax.numpy as jnp
from jax import lax
from jax.experimental import pallas as pl
from jax.experimental.pallas import tpu as pltpu
from jax.sharding import PartitionSpec as P

MESH = pl.DeviceIdType.MESH
LANES = 512
GROUP = 4


def kernel(
    dims, x_hbm, amp_hbm, virt_hbm, win_hbm, occ_hbm, pairs_hbm, out_ref,
    x_ref, amp_ref, virt_ref, win_ref, occ_ref, pairs_ref, local,
    a_buf, b_buf, transit, w_buf, wide, integral, parts, sums, inbox,
    near_send, mate_send, chain_send, a_recv, side_send, cross_send, fan_send, cross_recv, b_recv,
    w_send, w_recv, r_send, r_recv,
):
    n_rows, n_cols, n_pairs, slab = dims
    row, col, pair = lax.axis_index("row"), lax.axis_index("col"), lax.axis_index("pair")
    width = amp_ref.shape[2]
    height = 2 * width
    n_fit = x_ref.shape[2]
    n_groups = n_cols // 2 // GROUP
    n_x = n_rows // 2
    core = lax.rem(col, 2)
    place = lax.rem(lax.div(col, 2), GROUP)
    group = lax.div(lax.div(col, 2), GROUP)
    upper = jnp.bitwise_and(row, 1) == 1

    def column(g, p):
        return (g * GROUP + p) * 2 + core

    def at(r=None, c=None, p=None):
        return (row if r is None else r, col if c is None else c, pair if p is None else p)

    near = [column(group, jnp.bitwise_xor(place, j)) for j in range(1, GROUP)]
    beside = near[0]
    mate = jnp.bitwise_xor(col, 1)
    half = jnp.bitwise_xor(row, 1)
    sides = [jnp.bitwise_xor(row, 2 * k) for k in range(1, n_x)]
    others = [jnp.bitwise_xor(pair, k) for k in range(1, n_pairs)]
    left, right = column(group - 1, place), column(group + 1, place)
    has_left, has_right = group > 0, group < n_groups - 1

    barrier = pltpu.get_barrier_semaphore()

    def greet(peer):
        pl.semaphore_signal(barrier, inc=1, device_id=peer, device_id_type=MESH)

    peers = [at(c=c) for c in near + [mate]] + [at(r=r) for r in sides] + [at(p=p) for p in others]
    peers += [at(r=r, c=beside) for r in sides]
    for peer in peers:
        greet(peer)
    pl.when(has_right)(lambda: greet(at(c=right)))
    pl.when(jnp.logical_not(upper))(lambda: greet(at(r=half, c=beside)))

    loads = []
    operands = (
        (x_hbm, x_ref), (amp_hbm, amp_ref), (win_hbm, win_ref), (occ_hbm, occ_ref), (pairs_hbm, pairs_ref),
        (virt_hbm, virt_ref),
    )
    for i, (src, dst) in enumerate(operands):
        loads.append(pltpu.make_async_copy(src, dst, local.at[i]))
        loads[i].start()

    loads[0].wait()
    own = jnp.concatenate([x_ref[0], x_ref[1]], axis=0)
    own = jnp.concatenate([own, jnp.zeros((height, LANES - n_fit), own.dtype)], axis=1)
    a_buf[col] = own
    b_buf[row] = own

    pl.semaphore_wait(barrier, len(peers) + jnp.where(has_left, 1, 0) + jnp.where(upper, 1, 0))

    def copy(src, dst, sent, landed, target):
        return pltpu.make_async_remote_copy(
            src_ref=src, dst_ref=dst, send_sem=sent, recv_sem=landed, device_id=target, device_id_type=MESH
        )

    def block(slot, sent, c):
        return copy(a_buf.at[slot], a_buf.at[slot], sent, a_recv.at[slot], at(c=c))

    def cross():
        return copy(a_buf.at[col], transit, cross_send, cross_recv, at(r=half, c=beside))

    def fan(i, r):
        return copy(transit, b_buf.at[half], fan_send.at[i], b_recv.at[half], at(r=r, c=beside))

    def side(i, r):
        return copy(b_buf.at[row], b_buf.at[row], side_send.at[i], b_recv.at[row], at(r=r))

    def near_copy(g, slot, j):
        return block(slot, near_send.at[g * (GROUP - 1) + j], near[j])

    def mate_copy(slot):
        return block(slot, mate_send.at[lax.div(slot, 2)], mate)

    def spread_block(g):
        slot = column(g, place)
        for j in range(GROUP - 1):
            near_copy(g, slot, j).start()
        mate_copy(slot).start()

    def chain(g, target, index):
        return block(column(g, place), chain_send.at[index], target)

    pl.when(upper)(lambda: cross().start())
    pl.when(has_left)(lambda: chain(group, left, n_groups).start())
    spread_block(group)
    for i, r in enumerate(sides):
        side(i, r).start()

    for load in loads[1:]:
        load.wait()
    symmetry = []
    for s in range(slab):
        first, second = pairs_ref[0, pair * slab + s], pairs_ref[1, pair * slab + s]
        symmetry.append(jnp.bitwise_xor(occ_ref[first], occ_ref[second]))
    down = lax.broadcasted_iota(jnp.int32, (width, width), 0)
    across = lax.broadcasted_iota(jnp.int32, (width, width), 1)
    product = jnp.zeros((width, width), jnp.int32)
    for j in range(width):
        label = win_ref[j]
        product = jnp.bitwise_xor(product, jnp.where(down == j, label, 0))
        product = jnp.bitwise_xor(product, jnp.where(across == j, label, 0))
    for s in range(slab):
        kept = jnp.where(product == symmetry[s], amp_ref[s].astype(jnp.float32), 0.0)
        w_buf[pair, s * width:(s + 1) * width, :] = kept.astype(jnp.bfloat16)

    def give_weights(i):
        return copy(w_buf.at[pair], w_buf.at[pair], w_send.at[i], w_recv.at[pair], at(p=others[i]))

    for i in range(len(others)):
        give_weights(i).start()

    n_b = n_x * 2
    span = n_b * width
    tall = slab * n_b
    line = lax.broadcasted_iota(jnp.int32, (2 * n_b, span), 0)
    lane = lax.broadcasted_iota(jnp.int32, (2 * n_b, span), 1)
    own_b = lax.div(lane, width) == lax.rem(line, n_b)
    spread = (
        lax.rem(lax.broadcasted_iota(jnp.int32, (width, span), 1), width)
        == lax.broadcasted_iota(jnp.int32, (width, span), 0)
    ).astype(jnp.bfloat16)

    def expand(p):
        def one(s, carry):
            lines = jnp.dot(
                w_buf[p, pl.ds(pl.multiple_of(s * 2 * width, 2 * width), 2 * width), :], spread,
                preferred_element_type=jnp.float32,
            )
            start = pl.multiple_of(p * tall + s * 2 * n_b, 2 * n_b)
            for c in range(width):
                first = jnp.broadcast_to(lines[c:c + 1, :], own_b.shape)
                second = jnp.broadcast_to(lines[width + c:width + c + 1, :], own_b.shape)
                tile = jnp.where(own_b, jnp.where(line < n_b, first, second), 0.0)
                wide[pl.ds(start, 2 * n_b), c * span:(c + 1) * span] = tile.astype(jnp.bfloat16)
            return carry

        lax.fori_loop(0, slab // 2, one, 0)

    expand(pair)

    def from_right(d):
        g = group + d
        block(column(g, place), chain_send.at[0], right).wait_recv()
        if d == 1:
            chain(group, right, n_groups + 1).start()
        pl.when(has_left)(lambda: chain(g, left, g).start())
        spread_block(g)

    def from_left(d):
        g = group - d
        block(column(g, place), chain_send.at[0], left).wait_recv()
        pl.when(has_right)(lambda: chain(g, right, g).start())
        spread_block(g)

    for d in range(1, n_groups):
        pl.when(group + d < n_groups)(functools.partial(from_right, d))
        pl.when(group - d >= 0)(functools.partial(from_left, d))
        if d == 1:
            for p in others:
                copy(w_buf.at[p], w_buf.at[p], w_send.at[0], w_recv.at[p], at(p=p)).wait_recv()
                expand(p)

    def handover(k, j):
        slot = column(jnp.bitwise_xor(group, k), jnp.bitwise_xor(place, j))
        block(slot, near_send.at[0], near[j - 1]).wait_recv()
        mate_copy(slot).start()

    def from_half():
        cross().wait_recv()
        pl.when(jnp.logical_not(upper))(lambda: cross().start())
        for i, r in enumerate([row] + sides):
            fan(i, r).start()

    for k in range(2):
        for j in range(1, GROUP):
            handover(k, j)
    pl.when(jnp.logical_not(upper))(from_half)
    for k in range(2, n_groups):
        for j in range(1, GROUP):
            handover(k, j)
    pl.when(upper)(from_half)
    for r in sides:
        copy(b_buf.at[r], b_buf.at[r], side_send.at[0], b_recv.at[r], at(r=r)).wait_recv()
    for c in range(n_cols // 2):
        block(2 * c + 1 - core, mate_send.at[0], mate).wait_recv()

    n_a = 2 * n_cols
    chunk = 8

    def contract(side_of, where):
        b_rows = jnp.concatenate([b_buf[2 * x + side_of] for x in range(n_x)], axis=0)

        def multiply(i, carry):
            first = pl.multiple_of(i * chunk, chunk)
            rows = a_buf[pl.ds(first, chunk)].reshape(chunk * height, LANES)
            integral[pl.ds(pl.multiple_of(first * height, chunk * height), chunk * height), :] = lax.dot_general(
                rows, b_rows, (((1,), (1,)), ((), ())), preferred_element_type=jnp.float32
            )
            return carry

        lax.fori_loop(0, n_cols // chunk, multiply, 0)
        for c in range(width):
            lines = integral[pl.ds(c, n_a, stride=width), :]
            high = lines.astype(jnp.bfloat16)
            parts[0:n_a, c * span:(c + 1) * span] = high
            parts[n_a:2 * n_a, c * span:(c + 1) * span] = (lines - high.astype(jnp.float32)).astype(jnp.bfloat16)

    def residual(p):
        both = lax.dot_general(
            wide[pl.ds(pl.multiple_of(p * tall, 2 * n_b), tall), :], parts[...], (((1,), (1,)), ((), ())),
            preferred_element_type=jnp.float32,
        )
        return both[:, 0:n_a] + both[:, n_a:2 * n_a]

    here = jnp.bitwise_and(row, 1)
    contract(here, 0)
    for p in others + [pair]:
        sums[p, :, 0:n_a] = residual(p)

    label_lane = lax.broadcasted_iota(jnp.int32, (n_b, 2 * n_a), 1)
    label_line = lax.broadcasted_iota(jnp.int32, (n_b, 2 * n_a), 0)
    label = jnp.zeros((n_b, 2 * n_a), jnp.int32)
    lane_a = lax.rem(label_lane, n_a)
    for j in range(n_a):
        label = jnp.where(lane_a == j, virt_ref[row * n_a + j], label)
    for x in range(n_x):
        for m in range(2):
            mine = virt_ref[(2 * x + here) * n_a + col * 2 + m]
            far = virt_ref[(2 * x + 1 - here) * n_a + col * 2 + m]
            there = jnp.where(label_lane < n_a, mine, far)
            label = jnp.bitwise_xor(label, jnp.where(label_line == 2 * x + m, there, 0))

    for i in range(n_x):
        r = jnp.bitwise_xor(half, 2 * i)
        copy(transit, b_buf.at[r], fan_send.at[0], b_recv.at[r], at(r=jnp.bitwise_xor(row, 2 * i), c=beside)).wait_recv()
    contract(1 - here, 1)

    def give_sum(i):
        return copy(sums.at[others[i]], inbox.at[pair], r_send.at[i], r_recv.at[pair], at(p=others[i]))

    for i, p in enumerate(others):
        sums[p, :, n_a:2 * n_a] = residual(p)
        give_sum(i).start()
    sums[pair, :, n_a:2 * n_a] = residual(pair)
    total = sums[pair]
    for p in others:
        copy(sums.at[p], inbox.at[p], r_send.at[0], r_recv.at[p], at(p=p)).wait_recv()
        total = total + inbox[p]
    for s in range(slab):
        kept = jnp.where(label == symmetry[s], total[s * n_b:(s + 1) * n_b], 0.0)
        mine, far = kept[:, 0:n_a], kept[:, n_a:2 * n_a]
        even, odd = jnp.where(upper, far, mine), jnp.where(upper, mine, far)
        for x in range(n_x):
            out_ref[s, 4 * x:4 * x + 2, :] = even[2 * x:2 * x + 2]
            out_ref[s, 4 * x + 2:4 * x + 4, :] = odd[2 * x:2 * x + 2]

    for g in range(n_groups):
        slot = column(g, place)
        for j in range(GROUP - 1):
            near_copy(g, slot, j).wait_send()
        pl.when(jnp.logical_or(jnp.logical_and(g > group, has_left), jnp.logical_and(g < group, has_right)))(
            functools.partial(lambda g: chain(g, left, g).wait_send(), g)
        )
    pl.when(has_left)(lambda: chain(group, left, n_groups).wait_send())
    pl.when(has_right)(lambda: chain(group, right, n_groups + 1).wait_send())
    for c in range(n_cols // 2):
        mate_copy(2 * c + core).wait_send()
    for i, r in enumerate(sides):
        side(i, r).wait_send()
    for i, r in enumerate([row] + sides):
        fan(i, r).wait_send()
    cross().wait_send()
    for i in range(len(others)):
        give_weights(i).wait_send()
        give_sum(i).wait_send()


def body(factors, amplitudes, virt_irreps, win_irreps, occ_irreps, pair_list):
    n_rows, n_cols, n_pairs = (lax.axis_size(name) for name in ("row", "col", "pair"))
    slab, width = amplitudes.shape[0], amplitudes.shape[1]
    per_device = factors.shape[1]
    n_a = per_device * n_cols
    n_x = n_rows // 2
    n_b = n_x * per_device
    span = n_b * width
    n_groups = n_cols // 2 // GROUP
    height = per_device * width
    hbm = pl.BlockSpec(memory_space=pltpu.HBM)
    dma = pltpu.SemaphoreType.DMA
    out = pl.pallas_call(
        functools.partial(kernel, (n_rows, n_cols, n_pairs, slab)),
        out_shape=jax.ShapeDtypeStruct((slab, n_rows * per_device, n_a), jnp.float32),
        in_specs=[hbm] * 6,
        out_specs=pl.BlockSpec(memory_space=pltpu.VMEM),
        scratch_shapes=[
            pltpu.VMEM((per_device, width, factors.shape[0]), factors.dtype),
            pltpu.VMEM(amplitudes.shape, amplitudes.dtype),
            pltpu.SMEM(virt_irreps.shape, jnp.int32),
            pltpu.SMEM(win_irreps.shape, jnp.int32),
            pltpu.SMEM(occ_irreps.shape, jnp.int32),
            pltpu.SMEM(pair_list.shape[::-1], jnp.int32),
            dma((6,)),
            pltpu.VMEM((n_cols, height, LANES), jnp.bfloat16),
            pltpu.VMEM((n_rows, height, LANES), jnp.bfloat16),
            pltpu.VMEM((height, LANES), jnp.bfloat16),
            pltpu.VMEM((n_pairs, slab * width, width), jnp.bfloat16),
            pltpu.VMEM((n_pairs * slab * n_b, width * span), jnp.bfloat16),
            pltpu.VMEM((n_a * width, span), jnp.float32),
            pltpu.VMEM((2 * n_a, width * span), jnp.bfloat16),
            pltpu.VMEM((n_pairs, slab * n_b, 2 * n_a), jnp.float32),
            pltpu.VMEM((n_pairs, slab * n_b, 2 * n_a), jnp.float32),
            dma((n_groups * (GROUP - 1),)), dma((n_cols // 2,)), dma((n_groups + 2,)), dma((n_cols,)),
            dma((n_x - 1,)), dma, dma((n_x,)), dma, dma((n_rows,)),
            dma((n_pairs,)), dma((n_pairs,)), dma((n_pairs,)), dma((n_pairs,)),
        ],
        compiler_params=pltpu.CompilerParams(
            collective_id=0, has_side_effects=True, vmem_limit_bytes=56 * 1024 * 1024
        ),
        name="ladder",
    )(jnp.transpose(factors, (1, 2, 0)), amplitudes, virt_irreps, win_irreps, occ_irreps, pair_list.T)
    return jnp.transpose(out.reshape(slab, n_rows, per_device, n_a), (0, 3, 1, 2))


def solution(mesh):
    in_specs = (P("pair", ("row", "col"), None), P("pair", None, None), P(), P(), P(), P())
    out_specs = P("pair", "row", None, "col")
    return jax.shard_map(body, mesh=mesh, in_specs=in_specs, out_specs=out_specs, check_vma=False)
```

```python
import functools

import jax
import jax.numpy as jnp
from jax import lax
from jax.experimental import pallas as pl
from jax.experimental.pallas import tpu as pltpu
from jax.sharding import PartitionSpec as P

MESH = pl.DeviceIdType.MESH
LANES = 512
GROUP = 4


def kernel(
    dims, x_hbm, amp_hbm, virt_hbm, win_hbm, occ_hbm, pairs_hbm, out_ref,
    x_ref, amp_ref, virt_ref, win_ref, occ_ref, pairs_ref, local,
    a_buf, b_buf, transit, w_buf, wide, integral, parts, sums, inbox,
    near_send, mate_send, chain_send, a_recv, side_send, cross_send, fan_send, cross_recv, b_recv,
    w_send, w_recv, r_send, r_recv, edge_send, ready,
):
    n_rows, n_cols, n_pairs, slab = dims
    row, col, pair = lax.axis_index("row"), lax.axis_index("col"), lax.axis_index("pair")
    width = amp_ref.shape[2]
    height = 2 * width
    n_fit = x_ref.shape[2]
    n_groups = n_cols // 2 // GROUP
    n_x = n_rows // 2
    core = lax.rem(col, 2)
    place = lax.rem(lax.div(col, 2), GROUP)
    group = lax.div(lax.div(col, 2), GROUP)
    upper = jnp.bitwise_and(row, 1) == 1

    def column(g, p):
        return (g * GROUP + p) * 2 + core

    def at(r=None, c=None, p=None):
        return (row if r is None else r, col if c is None else c, pair if p is None else p)

    near = [column(group, jnp.bitwise_xor(place, j)) for j in range(1, GROUP)]
    beside = near[0]
    mate = jnp.bitwise_xor(col, 1)
    half = jnp.bitwise_xor(row, 1)
    sides = [jnp.bitwise_xor(row, 2 * k) for k in range(1, n_x)]
    others = [jnp.bitwise_xor(pair, k) for k in range(1, n_pairs)]
    left, right = column(group - 1, place), column(group + 1, place)
    has_left, has_right = group > 0, group < n_groups - 1
    lower = jnp.logical_not(upper)
    at_first, at_last = jnp.logical_not(has_left), jnp.logical_not(has_right)
    direct_out = jnp.logical_and(upper, has_right)
    direct_in = jnp.logical_and(lower, has_right)
    edge = jnp.logical_or(at_first, at_last)
    low_edge, high_edge = jnp.logical_and(lower, edge), jnp.logical_and(upper, edge)
    opposite = column(n_groups - 1 - group, place)
    inner = jnp.where(at_first, column(1, place), column(n_groups - 2, place))

    barrier = pltpu.get_barrier_semaphore()

    def greet(peer):
        pl.semaphore_signal(barrier, inc=1, device_id=peer, device_id_type=MESH)

    peers = [at(c=c) for c in near + [mate]] + [at(r=r) for r in sides] + [at(p=p) for p in others]
    peers += [at(r=r, c=beside) for r in sides]
    for peer in peers:
        greet(peer)
    pl.when(has_right)(lambda: greet(at(c=right)))
    pl.when(jnp.logical_and(upper, has_left))(lambda: greet(at(c=left)))
    pl.when(low_edge)(lambda: greet(at(r=half, c=opposite)))
    pl.when(direct_in)(lambda: greet(at(r=half, c=beside)))

    loads = []
    operands = (
        (x_hbm, x_ref), (amp_hbm, amp_ref), (win_hbm, win_ref), (occ_hbm, occ_ref), (pairs_hbm, pairs_ref),
        (virt_hbm, virt_ref),
    )
    for i, (src, dst) in enumerate(operands):
        loads.append(pltpu.make_async_copy(src, dst, local.at[i]))
        loads[i].start()

    loads[0].wait()
    own = jnp.concatenate([x_ref[0], x_ref[1]], axis=0)
    own = jnp.concatenate([own, jnp.zeros((height, LANES - n_fit), own.dtype)], axis=1)
    a_buf[col] = own
    b_buf[row] = own

    awaited = len(peers) + jnp.where(has_left, 1, 0) + jnp.where(direct_out, 2, 0) + jnp.where(high_edge, 1, 0)
    pl.semaphore_wait(barrier, awaited)
    pl.when(high_edge)(
        lambda: pl.semaphore_signal(ready, inc=1, device_id=at(r=half, c=opposite), device_id_type=MESH)
    )

    def copy(src, dst, sent, landed, target):
        return pltpu.make_async_remote_copy(
            src_ref=src, dst_ref=dst, send_sem=sent, recv_sem=landed, device_id=target, device_id_type=MESH
        )

    def block(slot, sent, c):
        return copy(a_buf.at[slot], a_buf.at[slot], sent, a_recv.at[slot], at(c=c))

    def cross():
        return copy(a_buf.at[col], transit, cross_send, cross_recv, at(r=half, c=beside))

    def fan(i, r):
        return copy(transit, b_buf.at[half], fan_send.at[i], b_recv.at[half], at(r=r, c=beside))

    def over(source, to_b, index):
        return copy(
            a_buf.at[source], b_buf.at[row] if to_b else transit, edge_send.at[index],
            b_recv.at[row] if to_b else cross_recv, at(r=half, c=opposite),
        )

    def inward():
        return copy(transit, b_buf.at[half], edge_send.at[0], b_recv.at[half], at(c=inner))

    def share(i, r):
        return copy(b_buf.at[half], b_buf.at[half], fan_send.at[i + 1], b_recv.at[half], at(r=r))

    def side(i, r):
        return copy(b_buf.at[row], b_buf.at[row], side_send.at[i], b_recv.at[row], at(r=r))

    def near_copy(g, slot, j):
        return block(slot, near_send.at[g * (GROUP - 1) + j], near[j])

    def mate_copy(slot):
        return block(slot, mate_send.at[lax.div(slot, 2)], mate)

    def spread_block(g):
        slot = column(g, place)
        for j in range(GROUP - 1):
            near_copy(g, slot, j).start()
        mate_copy(slot).start()

    def chain(g, target, index):
        return block(column(g, place), chain_send.at[index], target)

    pl.when(direct_out)(lambda: cross().start())
    pl.when(has_left)(lambda: chain(group, left, n_groups).start())
    pl.when(jnp.logical_and(upper, has_right))(lambda: chain(group, right, n_groups + 1).start())
    spread_block(group)
    for i, r in enumerate(sides):
        side(i, r).start()

    for load in loads[1:]:
        load.wait()
    symmetry = []
    for s in range(slab):
        first, second = pairs_ref[0, pair * slab + s], pairs_ref[1, pair * slab + s]
        symmetry.append(jnp.bitwise_xor(occ_ref[first], occ_ref[second]))
    down = lax.broadcasted_iota(jnp.int32, (width, width), 0)
    across = lax.broadcasted_iota(jnp.int32, (width, width), 1)
    product = jnp.zeros((width, width), jnp.int32)
    for j in range(width):
        label = win_ref[j]
        product = jnp.bitwise_xor(product, jnp.where(down == j, label, 0))
        product = jnp.bitwise_xor(product, jnp.where(across == j, label, 0))
    for s in range(slab):
        kept = jnp.where(product == symmetry[s], amp_ref[s].astype(jnp.float32), 0.0)
        w_buf[pair, s * width:(s + 1) * width, :] = kept.astype(jnp.bfloat16)

    def give_weights(i):
        return copy(w_buf.at[pair], w_buf.at[pair], w_send.at[i], w_recv.at[pair], at(p=others[i]))

    for i in range(len(others)):
        give_weights(i).start()

    n_b = n_x * 2
    span = n_b * width
    tall = slab * n_b
    line = lax.broadcasted_iota(jnp.int32, (2 * n_b, span), 0)
    lane = lax.broadcasted_iota(jnp.int32, (2 * n_b, span), 1)
    own_b = lax.div(lane, width) == lax.rem(line, n_b)
    spread = (
        lax.rem(lax.broadcasted_iota(jnp.int32, (width, span), 1), width)
        == lax.broadcasted_iota(jnp.int32, (width, span), 0)
    ).astype(jnp.bfloat16)

    def expand(p):
        def one(s, carry):
            lines = jnp.dot(
                w_buf[p, pl.ds(pl.multiple_of(s * 2 * width, 2 * width), 2 * width), :], spread,
                preferred_element_type=jnp.float32,
            )
            start = pl.multiple_of(p * tall + s * 2 * n_b, 2 * n_b)
            for c in range(width):
                first = jnp.broadcast_to(lines[c:c + 1, :], own_b.shape)
                second = jnp.broadcast_to(lines[width + c:width + c + 1, :], own_b.shape)
                tile = jnp.where(own_b, jnp.where(line < n_b, first, second), 0.0)
                wide[pl.ds(start, 2 * n_b), c * span:(c + 1) * span] = tile.astype(jnp.bfloat16)
            return carry

        lax.fori_loop(0, slab // 2, one, 0)

    expand(pair)

    def onward(d, g):
        if d == n_groups - 2:
            pl.semaphore_wait(ready, 1)
        over(column(g, place), d == n_groups - 1, d - (n_groups - 2)).start()

    def from_right(d):
        g = group + d
        block(column(g, place), chain_send.at[0], right).wait_recv()
        if d == 1:
            pl.when(lower)(lambda: chain(group, right, n_groups + 1).start())
        pl.when(has_left)(lambda: chain(g, left, g).start())
        if d >= n_groups - 2:
            pl.when(jnp.logical_and(at_first, lower))(lambda: onward(d, g))
        if d == n_groups - 1:
            pl.when(jnp.logical_and(upper, at_first))(lambda: over(column(g, place), True, 1).start())
        spread_block(g)

    def from_left(d):
        g = group - d
        block(column(g, place), chain_send.at[0], left).wait_recv()
        pl.when(has_right)(lambda: chain(g, right, g).start())
        if d >= n_groups - 2:
            pl.when(jnp.logical_and(at_last, lower))(lambda: onward(d, g))
        spread_block(g)

    for d in range(1, n_groups):
        pl.when(group + d < n_groups)(functools.partial(from_right, d))
        pl.when(group - d >= 0)(functools.partial(from_left, d))
        if d == 1:
            for p in others:
                copy(w_buf.at[p], w_buf.at[p], w_send.at[0], w_recv.at[p], at(p=p)).wait_recv()
                expand(p)

    def handover(k, j):
        slot = column(jnp.bitwise_xor(group, k), jnp.bitwise_xor(place, j))
        block(slot, near_send.at[0], near[j - 1]).wait_recv()
        mate_copy(slot).start()

    def turn_in():
        cross().wait_recv()
        inward().start()

    def from_direct():
        cross().wait_recv()
        for i, r in enumerate([row] + sides):
            fan(i, r).start()

    def from_chain():
        share(0, row).wait_recv()
        for i, r in enumerate(sides):
            share(i, r).start()

    pl.when(high_edge)(turn_in)
    pl.when(direct_in)(from_direct)
    for k in range(n_groups):
        for j in range(1, GROUP):
            handover(k, j)
    pl.when(jnp.logical_not(direct_in))(from_chain)
    for r in sides:
        copy(b_buf.at[r], b_buf.at[r], side_send.at[0], b_recv.at[r], at(r=r)).wait_recv()
    for c in range(n_cols // 2):
        block(2 * c + 1 - core, mate_send.at[0], mate).wait_recv()

    n_a = 2 * n_cols
    chunk = 8

    def contract(side_of, where):
        b_rows = jnp.concatenate([b_buf[2 * x + side_of] for x in range(n_x)], axis=0)

        def multiply(i, carry):
            first = pl.multiple_of(i * chunk, chunk)
            rows = a_buf[pl.ds(first, chunk)].reshape(chunk * height, LANES)
            integral[pl.ds(pl.multiple_of(first * height, chunk * height), chunk * height), :] = lax.dot_general(
                rows, b_rows, (((1,), (1,)), ((), ())), preferred_element_type=jnp.float32
            )
            return carry

        lax.fori_loop(0, n_cols // chunk, multiply, 0)
        for c in range(width):
            lines = integral[pl.ds(c, n_a, stride=width), :]
            high = lines.astype(jnp.bfloat16)
            parts[0:n_a, c * span:(c + 1) * span] = high
            parts[n_a:2 * n_a, c * span:(c + 1) * span] = (lines - high.astype(jnp.float32)).astype(jnp.bfloat16)

    def residual(p):
        both = lax.dot_general(
            wide[pl.ds(pl.multiple_of(p * tall, 2 * n_b), tall), :], parts[...], (((1,), (1,)), ((), ())),
            preferred_element_type=jnp.float32,
        )
        return both[:, 0:n_a] + both[:, n_a:2 * n_a]

    here = jnp.bitwise_and(row, 1)
    contract(here, 0)
    for p in others + [pair]:
        sums[p, :, 0:n_a] = residual(p)

    label_lane = lax.broadcasted_iota(jnp.int32, (n_b, 2 * n_a), 1)
    label_line = lax.broadcasted_iota(jnp.int32, (n_b, 2 * n_a), 0)
    label = jnp.zeros((n_b, 2 * n_a), jnp.int32)
    lane_a = lax.rem(label_lane, n_a)
    for j in range(n_a):
        label = jnp.where(lane_a == j, virt_ref[row * n_a + j], label)
    for x in range(n_x):
        for m in range(2):
            mine = virt_ref[(2 * x + here) * n_a + col * 2 + m]
            far = virt_ref[(2 * x + 1 - here) * n_a + col * 2 + m]
            there = jnp.where(label_lane < n_a, mine, far)
            label = jnp.bitwise_xor(label, jnp.where(label_line == 2 * x + m, there, 0))

    def half_arrived(i):
        slot = jnp.bitwise_xor(half, 2 * i)
        copy(b_buf.at[slot], b_buf.at[slot], fan_send.at[0], b_recv.at[slot], at(r=half, c=beside)).wait_recv()

    pl.when(direct_in)(lambda: half_arrived(0))
    for i in range(1, n_x):
        half_arrived(i)
    contract(1 - here, 1)

    def give_sum(i):
        return copy(sums.at[others[i]], inbox.at[pair], r_send.at[i], r_recv.at[pair], at(p=others[i]))

    for i, p in enumerate(others):
        sums[p, :, n_a:2 * n_a] = residual(p)
        give_sum(i).start()
    sums[pair, :, n_a:2 * n_a] = residual(pair)
    total = sums[pair]
    for p in others:
        copy(sums.at[p], inbox.at[p], r_send.at[0], r_recv.at[p], at(p=p)).wait_recv()
        total = total + inbox[p]
    for s in range(slab):
        kept = jnp.where(label == symmetry[s], total[s * n_b:(s + 1) * n_b], 0.0)
        mine, far = kept[:, 0:n_a], kept[:, n_a:2 * n_a]
        even, odd = jnp.where(upper, far, mine), jnp.where(upper, mine, far)
        for x in range(n_x):
            out_ref[s, 4 * x:4 * x + 2, :] = even[2 * x:2 * x + 2]
            out_ref[s, 4 * x + 2:4 * x + 4, :] = odd[2 * x:2 * x + 2]

    for g in range(n_groups):
        slot = column(g, place)
        for j in range(GROUP - 1):
            near_copy(g, slot, j).wait_send()
        pl.when(jnp.logical_or(jnp.logical_and(g > group, has_left), jnp.logical_and(g < group, has_right)))(
            functools.partial(lambda g: chain(g, left, g).wait_send(), g)
        )
    pl.when(has_left)(lambda: chain(group, left, n_groups).wait_send())
    pl.when(has_right)(lambda: chain(group, right, n_groups + 1).wait_send())
    for c in range(n_cols // 2):
        mate_copy(2 * c + core).wait_send()
    for i, r in enumerate(sides):
        side(i, r).wait_send()
    pl.when(direct_in)(lambda: fan(0, row).wait_send())
    for i, r in enumerate(sides):
        share(i, r).wait_send()
    pl.when(direct_out)(lambda: cross().wait_send())
    pl.when(low_edge)(lambda: over(col, False, 0).wait_send())
    pl.when(low_edge)(lambda: over(col, True, 1).wait_send())
    pl.when(jnp.logical_and(upper, at_first))(lambda: over(col, True, 1).wait_send())
    pl.when(high_edge)(lambda: inward().wait_send())
    for i in range(len(others)):
        give_weights(i).wait_send()
        give_sum(i).wait_send()


def body(factors, amplitudes, virt_irreps, win_irreps, occ_irreps, pair_list):
    n_rows, n_cols, n_pairs = (lax.axis_size(name) for name in ("row", "col", "pair"))
    slab, width = amplitudes.shape[0], amplitudes.shape[1]
    per_device = factors.shape[1]
    n_a = per_device * n_cols
    n_x = n_rows // 2
    n_b = n_x * per_device
    span = n_b * width
    n_groups = n_cols // 2 // GROUP
    height = per_device * width
    hbm = pl.BlockSpec(memory_space=pltpu.HBM)
    dma = pltpu.SemaphoreType.DMA
    out = pl.pallas_call(
        functools.partial(kernel, (n_rows, n_cols, n_pairs, slab)),
        out_shape=jax.ShapeDtypeStruct((slab, n_rows * per_device, n_a), jnp.float32),
        in_specs=[hbm] * 6,
        out_specs=pl.BlockSpec(memory_space=pltpu.VMEM),
        scratch_shapes=[
            pltpu.VMEM((per_device, width, factors.shape[0]), factors.dtype),
            pltpu.VMEM(amplitudes.shape, amplitudes.dtype),
            pltpu.SMEM(virt_irreps.shape, jnp.int32),
            pltpu.SMEM(win_irreps.shape, jnp.int32),
            pltpu.SMEM(occ_irreps.shape, jnp.int32),
            pltpu.SMEM(pair_list.shape[::-1], jnp.int32),
            dma((6,)),
            pltpu.VMEM((n_cols, height, LANES), jnp.bfloat16),
            pltpu.VMEM((n_rows, height, LANES), jnp.bfloat16),
            pltpu.VMEM((height, LANES), jnp.bfloat16),
            pltpu.VMEM((n_pairs, slab * width, width), jnp.bfloat16),
            pltpu.VMEM((n_pairs * slab * n_b, width * span), jnp.bfloat16),
            pltpu.VMEM((n_a * width, span), jnp.float32),
            pltpu.VMEM((2 * n_a, width * span), jnp.bfloat16),
            pltpu.VMEM((n_pairs, slab * n_b, 2 * n_a), jnp.float32),
            pltpu.VMEM((n_pairs, slab * n_b, 2 * n_a), jnp.float32),
            dma((n_groups * (GROUP - 1),)), dma((n_cols // 2,)), dma((n_groups + 2,)), dma((n_cols,)),
            dma((n_x - 1,)), dma, dma((n_x,)), dma, dma((n_rows,)),
            dma((n_pairs,)), dma((n_pairs,)), dma((n_pairs,)), dma((n_pairs,)), dma((2,)),
            pltpu.SemaphoreType.REGULAR,
        ],
        compiler_params=pltpu.CompilerParams(
            collective_id=0, has_side_effects=True, vmem_limit_bytes=56 * 1024 * 1024
        ),
        name="ladder",
    )(jnp.transpose(factors, (1, 2, 0)), amplitudes, virt_irreps, win_irreps, occ_irreps, pair_list.T)
    return jnp.transpose(out.reshape(slab, n_rows, per_device, n_a), (0, 3, 1, 2))


def solution(mesh):
    in_specs = (P("pair", ("row", "col"), None), P("pair", None, None), P(), P(), P(), P())
    out_specs = P("pair", "row", None, "col")
    return jax.shard_map(body, mesh=mesh, in_specs=in_specs, out_specs=out_specs, check_vma=False)
```

```python
import functools

import jax
import jax.numpy as jnp
from jax import lax
from jax.experimental import pallas as pl
from jax.experimental.pallas import tpu as pltpu
from jax.sharding import PartitionSpec as P

MESH = pl.DeviceIdType.MESH
LANES = 512
GROUP = 4


def kernel(
    dims, x_hbm, amp_hbm, virt_hbm, win_hbm, occ_hbm, pairs_hbm, out_ref,
    x_ref, amp_ref, virt_ref, win_ref, occ_ref, pairs_ref, local,
    a_buf, b_buf, transit, w_buf, wide, integral, parts, sums, inbox,
    near_send, mate_send, chain_send, a_recv, side_send, cross_send, fan_send, cross_recv, b_recv,
    w_send, w_recv, r_send, r_recv, edge_send, ready,
):
    n_rows, n_cols, n_pairs, slab = dims
    row, col, pair = lax.axis_index("row"), lax.axis_index("col"), lax.axis_index("pair")
    width = amp_ref.shape[2]
    height = 2 * width
    n_fit = x_ref.shape[2]
    n_groups = n_cols // 2 // GROUP
    n_x = n_rows // 2
    core = lax.rem(col, 2)
    place = lax.rem(lax.div(col, 2), GROUP)
    group = lax.div(lax.div(col, 2), GROUP)
    upper = jnp.bitwise_and(row, 1) == 1

    def column(g, p):
        return (g * GROUP + p) * 2 + core

    def at(r=None, c=None, p=None):
        return (row if r is None else r, col if c is None else c, pair if p is None else p)

    near = [column(group, jnp.bitwise_xor(place, j)) for j in range(1, GROUP)]
    beside = near[0]
    mate = jnp.bitwise_xor(col, 1)
    half = jnp.bitwise_xor(row, 1)
    sides = [jnp.bitwise_xor(row, 2 * k) for k in range(1, n_x)]
    others = [jnp.bitwise_xor(pair, k) for k in range(1, n_pairs)]
    left, right = column(group - 1, place), column(group + 1, place)
    has_left, has_right = group > 0, group < n_groups - 1
    lower = jnp.logical_not(upper)
    at_first, at_last = jnp.logical_not(has_left), jnp.logical_not(has_right)
    direct_out = jnp.logical_and(upper, has_right)
    direct_in = jnp.logical_and(lower, has_right)
    edge = jnp.logical_or(at_first, at_last)
    low_edge, high_edge = jnp.logical_and(lower, edge), jnp.logical_and(upper, edge)
    leap = jnp.logical_and(lower, group >= 2)
    passes_left = jnp.logical_and(has_left, jnp.logical_or(upper, group >= 2))
    opposite = column(n_groups - 1 - group, place)
    inner = jnp.where(at_first, column(1, place), column(n_groups - 2, place))

    barrier = pltpu.get_barrier_semaphore()

    def greet(peer):
        pl.semaphore_signal(barrier, inc=1, device_id=peer, device_id_type=MESH)

    peers = [at(c=c) for c in near + [mate]] + [at(r=r) for r in sides] + [at(p=p) for p in others]
    peers += [at(r=r, c=beside) for r in sides]
    for peer in peers:
        greet(peer)
    pl.when(has_right)(lambda: greet(at(c=right)))
    pl.when(jnp.logical_and(upper, has_left))(lambda: greet(at(c=left)))
    for g in range(2, n_groups):
        pl.when(jnp.logical_and(lower, at_first))(functools.partial(greet, at(c=column(g, place))))
    pl.when(low_edge)(lambda: greet(at(r=half, c=opposite)))
    pl.when(direct_in)(lambda: greet(at(r=half, c=beside)))

    loads = []
    operands = (
        (x_hbm, x_ref), (amp_hbm, amp_ref), (win_hbm, win_ref), (occ_hbm, occ_ref), (pairs_hbm, pairs_ref),
        (virt_hbm, virt_ref),
    )
    for i, (src, dst) in enumerate(operands):
        loads.append(pltpu.make_async_copy(src, dst, local.at[i]))
        loads[i].start()

    loads[0].wait()
    own = jnp.concatenate([x_ref[0], x_ref[1]], axis=0)
    own = jnp.concatenate([own, jnp.zeros((height, LANES - n_fit), own.dtype)], axis=1)
    a_buf[col] = own
    b_buf[row] = own

    awaited = len(peers) + jnp.where(has_left, 1, 0) + jnp.where(direct_out, 2, 0) + jnp.where(high_edge, 1, 0)
    awaited = awaited + jnp.where(leap, 1, 0)
    pl.semaphore_wait(barrier, awaited)
    pl.when(high_edge)(
        lambda: pl.semaphore_signal(ready, inc=1, device_id=at(r=half, c=opposite), device_id_type=MESH)
    )

    def copy(src, dst, sent, landed, target):
        return pltpu.make_async_remote_copy(
            src_ref=src, dst_ref=dst, send_sem=sent, recv_sem=landed, device_id=target, device_id_type=MESH
        )

    def block(slot, sent, c):
        return copy(a_buf.at[slot], a_buf.at[slot], sent, a_recv.at[slot], at(c=c))

    def cross():
        return copy(a_buf.at[col], transit, cross_send, cross_recv, at(r=half, c=beside))

    def fan(i, r):
        return copy(transit, b_buf.at[half], fan_send.at[i], b_recv.at[half], at(r=r, c=beside))

    def over(source, to_b, index):
        return copy(
            a_buf.at[source], b_buf.at[row] if to_b else transit, edge_send.at[index],
            b_recv.at[row] if to_b else cross_recv, at(r=half, c=opposite),
        )

    def inward():
        return copy(transit, b_buf.at[half], edge_send.at[0], b_recv.at[half], at(c=inner))

    def share(i, r):
        return copy(b_buf.at[half], b_buf.at[half], fan_send.at[i + 1], b_recv.at[half], at(r=r))

    def side(i, r):
        return copy(b_buf.at[row], b_buf.at[row], side_send.at[i], b_recv.at[row], at(r=r))

    def near_copy(g, slot, j):
        return block(slot, near_send.at[g * (GROUP - 1) + j], near[j])

    def mate_copy(slot):
        return block(slot, mate_send.at[lax.div(slot, 2)], mate)

    def spread_block(g):
        slot = column(g, place)
        for j in range(GROUP - 1):
            near_copy(g, slot, j).start()
        mate_copy(slot).start()

    def chain(g, target, index):
        return block(column(g, place), chain_send.at[index], target)

    pl.when(direct_out)(lambda: cross().start())
    pl.when(leap)(lambda: chain(group, column(0, place), n_groups + 2).start())
    pl.when(has_left)(lambda: chain(group, left, n_groups).start())
    pl.when(jnp.logical_and(upper, has_right))(lambda: chain(group, right, n_groups + 1).start())
    spread_block(group)
    for i, r in enumerate(sides):
        side(i, r).start()

    for load in loads[1:]:
        load.wait()
    symmetry = []
    for s in range(slab):
        first, second = pairs_ref[0, pair * slab + s], pairs_ref[1, pair * slab + s]
        symmetry.append(jnp.bitwise_xor(occ_ref[first], occ_ref[second]))
    down = lax.broadcasted_iota(jnp.int32, (width, width), 0)
    across = lax.broadcasted_iota(jnp.int32, (width, width), 1)
    product = jnp.zeros((width, width), jnp.int32)
    for j in range(width):
        label = win_ref[j]
        product = jnp.bitwise_xor(product, jnp.where(down == j, label, 0))
        product = jnp.bitwise_xor(product, jnp.where(across == j, label, 0))
    for s in range(slab):
        kept = jnp.where(product == symmetry[s], amp_ref[s].astype(jnp.float32), 0.0)
        w_buf[pair, s * width:(s + 1) * width, :] = kept.astype(jnp.bfloat16)

    def give_weights(i):
        return copy(w_buf.at[pair], w_buf.at[pair], w_send.at[i], w_recv.at[pair], at(p=others[i]))

    for i in range(len(others)):
        give_weights(i).start()

    n_b = n_x * 2
    span = n_b * width
    tall = slab * n_b
    line = lax.broadcasted_iota(jnp.int32, (2 * n_b, span), 0)
    lane = lax.broadcasted_iota(jnp.int32, (2 * n_b, span), 1)
    own_b = lax.div(lane, width) == lax.rem(line, n_b)
    spread = (
        lax.rem(lax.broadcasted_iota(jnp.int32, (width, span), 1), width)
        == lax.broadcasted_iota(jnp.int32, (width, span), 0)
    ).astype(jnp.bfloat16)

    def expand(p):
        def one(s, carry):
            lines = jnp.dot(
                w_buf[p, pl.ds(pl.multiple_of(s * 2 * width, 2 * width), 2 * width), :], spread,
                preferred_element_type=jnp.float32,
            )
            start = pl.multiple_of(p * tall + s * 2 * n_b, 2 * n_b)
            for c in range(width):
                first = jnp.broadcast_to(lines[c:c + 1, :], own_b.shape)
                second = jnp.broadcast_to(lines[width + c:width + c + 1, :], own_b.shape)
                tile = jnp.where(own_b, jnp.where(line < n_b, first, second), 0.0)
                wide[pl.ds(start, 2 * n_b), c * span:(c + 1) * span] = tile.astype(jnp.bfloat16)
            return carry

        lax.fori_loop(0, slab // 2, one, 0)

    expand(pair)

    def onward(d, g):
        if d == n_groups - 2:
            pl.semaphore_wait(ready, 1)
        over(column(g, place), d == n_groups - 1, d - (n_groups - 2)).start()

    def from_right(d):
        g = group + d
        block(column(g, place), chain_send.at[0], right).wait_recv()
        if d == 1:
            pl.when(lower)(lambda: chain(group, right, n_groups + 1).start())
        pl.when(passes_left)(lambda: chain(g, left, g).start())
        if d >= n_groups - 2:
            pl.when(jnp.logical_and(at_first, lower))(lambda: onward(d, g))
        if d == n_groups - 1:
            pl.when(jnp.logical_and(upper, at_first))(lambda: over(column(g, place), True, 1).start())
        spread_block(g)

    def from_left(d):
        g = group - d
        block(column(g, place), chain_send.at[0], left).wait_recv()
        pl.when(has_right)(lambda: chain(g, right, g).start())
        if d >= n_groups - 2:
            pl.when(jnp.logical_and(at_last, lower))(lambda: onward(d, g))
        spread_block(g)

    for d in range(1, n_groups):
        pl.when(group + d < n_groups)(functools.partial(from_right, d))
        pl.when(group - d >= 0)(functools.partial(from_left, d))
        if d == 1:
            for p in others:
                copy(w_buf.at[p], w_buf.at[p], w_send.at[0], w_recv.at[p], at(p=p)).wait_recv()
                expand(p)

    def handover(k, j):
        slot = column(jnp.bitwise_xor(group, k), jnp.bitwise_xor(place, j))
        block(slot, near_send.at[0], near[j - 1]).wait_recv()
        mate_copy(slot).start()

    def turn_in():
        cross().wait_recv()
        inward().start()

    def from_direct():
        cross().wait_recv()
        for i, r in enumerate([row] + sides):
            fan(i, r).start()

    def from_chain():
        share(0, row).wait_recv()
        for i, r in enumerate(sides):
            share(i, r).start()

    pl.when(high_edge)(turn_in)
    pl.when(direct_in)(from_direct)
    for k in range(n_groups):
        for j in range(1, GROUP):
            handover(k, j)
    pl.when(jnp.logical_not(direct_in))(from_chain)
    for r in sides:
        copy(b_buf.at[r], b_buf.at[r], side_send.at[0], b_recv.at[r], at(r=r)).wait_recv()
    here = jnp.bitwise_and(row, 1)
    n_a = 2 * n_cols
    label_lane = lax.broadcasted_iota(jnp.int32, (n_b, 2 * n_a), 1)
    label_line = lax.broadcasted_iota(jnp.int32, (n_b, 2 * n_a), 0)
    label = jnp.zeros((n_b, 2 * n_a), jnp.int32)
    lane_a = lax.rem(label_lane, n_a)
    for j in range(n_a):
        label = jnp.where(lane_a == j, virt_ref[row * n_a + j], label)
    for x in range(n_x):
        for m in range(2):
            mine = virt_ref[(2 * x + here) * n_a + col * 2 + m]
            far = virt_ref[(2 * x + 1 - here) * n_a + col * 2 + m]
            there = jnp.where(label_lane < n_a, mine, far)
            label = jnp.bitwise_xor(label, jnp.where(label_line == 2 * x + m, there, 0))

    def half_arrived(i):
        slot = jnp.bitwise_xor(half, 2 * i)
        copy(b_buf.at[slot], b_buf.at[slot], fan_send.at[0], b_recv.at[slot], at(r=half, c=beside)).wait_recv()

    pl.when(direct_in)(lambda: half_arrived(0))
    for i in range(1, n_x):
        half_arrived(i)
    b_rows = jnp.concatenate(
        [b_buf[2 * x + here] for x in range(n_x)] + [b_buf[2 * x + 1 - here] for x in range(n_x)], axis=0
    )
    deep = 2 * GROUP * height
    a_part = 2 * GROUP * 2

    def contract(k):
        g = jnp.bitwise_xor(group, k)
        for p in range(GROUP):
            slot = (g * GROUP + p) * 2 + 1 - core
            block(slot, mate_send.at[0], mate).wait_recv()
        rows = a_buf[pl.ds(pl.multiple_of(g * 2 * GROUP, 2 * GROUP), 2 * GROUP)].reshape(deep, LANES)
        tile = lax.dot_general(rows, b_rows, (((1,), (1,)), ((), ())), preferred_element_type=jnp.float32)
        for t in range(2):
            integral[t] = tile[:, t * span:(t + 1) * span]
            start = pl.multiple_of(t * n_a + g * a_part, a_part)
            for c in range(width):
                lines = integral[t, pl.ds(c, a_part, stride=width), :]
                high = lines.astype(jnp.bfloat16)
                low = (lines - high.astype(jnp.float32)).astype(jnp.bfloat16)
                parts[pl.ds(start, a_part), c * span:(c + 1) * span] = high
                parts[pl.ds(pl.multiple_of(2 * n_a + start, a_part), a_part), c * span:(c + 1) * span] = low

    for k in range(n_groups):
        contract(k)

    def residual(p):
        both = lax.dot_general(
            wide[pl.ds(pl.multiple_of(p * tall, 2 * n_b), tall), :], parts[...], (((1,), (1,)), ((), ())),
            preferred_element_type=jnp.float32,
        )
        return both[:, 0:2 * n_a] + both[:, 2 * n_a:4 * n_a]

    def give_sum(i):
        return copy(sums.at[others[i]], inbox.at[pair], r_send.at[i], r_recv.at[pair], at(p=others[i]))

    for i, p in enumerate(others):
        sums[p] = residual(p)
        give_sum(i).start()
    total = residual(pair)
    for p in others:
        copy(sums.at[p], inbox.at[p], r_send.at[0], r_recv.at[p], at(p=p)).wait_recv()
        total = total + inbox[p]
    for s in range(slab):
        kept = jnp.where(label == symmetry[s], total[s * n_b:(s + 1) * n_b], 0.0)
        mine, far = kept[:, 0:n_a], kept[:, n_a:2 * n_a]
        even, odd = jnp.where(upper, far, mine), jnp.where(upper, mine, far)
        for x in range(n_x):
            out_ref[s, 4 * x:4 * x + 2, :] = even[2 * x:2 * x + 2]
            out_ref[s, 4 * x + 2:4 * x + 4, :] = odd[2 * x:2 * x + 2]

    for g in range(n_groups):
        slot = column(g, place)
        for j in range(GROUP - 1):
            near_copy(g, slot, j).wait_send()
        pl.when(jnp.logical_or(jnp.logical_and(g > group, passes_left), jnp.logical_and(g < group, has_right)))(
            functools.partial(lambda g: chain(g, left, g).wait_send(), g)
        )
    pl.when(has_left)(lambda: chain(group, left, n_groups).wait_send())
    pl.when(leap)(lambda: chain(group, left, n_groups + 2).wait_send())
    pl.when(has_right)(lambda: chain(group, right, n_groups + 1).wait_send())
    for c in range(n_cols // 2):
        mate_copy(2 * c + core).wait_send()
    for i, r in enumerate(sides):
        side(i, r).wait_send()
    pl.when(direct_in)(lambda: fan(0, row).wait_send())
    for i, r in enumerate(sides):
        share(i, r).wait_send()
    pl.when(direct_out)(lambda: cross().wait_send())
    pl.when(low_edge)(lambda: over(col, False, 0).wait_send())
    pl.when(low_edge)(lambda: over(col, True, 1).wait_send())
    pl.when(jnp.logical_and(upper, at_first))(lambda: over(col, True, 1).wait_send())
    pl.when(high_edge)(lambda: inward().wait_send())
    for i in range(len(others)):
        give_weights(i).wait_send()
        give_sum(i).wait_send()


def body(factors, amplitudes, virt_irreps, win_irreps, occ_irreps, pair_list):
    n_rows, n_cols, n_pairs = (lax.axis_size(name) for name in ("row", "col", "pair"))
    slab, width = amplitudes.shape[0], amplitudes.shape[1]
    per_device = factors.shape[1]
    n_a = per_device * n_cols
    n_x = n_rows // 2
    n_b = n_x * per_device
    span = n_b * width
    n_groups = n_cols // 2 // GROUP
    height = per_device * width
    hbm = pl.BlockSpec(memory_space=pltpu.HBM)
    dma = pltpu.SemaphoreType.DMA
    out = pl.pallas_call(
        functools.partial(kernel, (n_rows, n_cols, n_pairs, slab)),
        out_shape=jax.ShapeDtypeStruct((slab, n_rows * per_device, n_a), jnp.float32),
        in_specs=[hbm] * 6,
        out_specs=pl.BlockSpec(memory_space=pltpu.VMEM),
        scratch_shapes=[
            pltpu.VMEM((per_device, width, factors.shape[0]), factors.dtype),
            pltpu.VMEM(amplitudes.shape, amplitudes.dtype),
            pltpu.SMEM(virt_irreps.shape, jnp.int32),
            pltpu.SMEM(win_irreps.shape, jnp.int32),
            pltpu.SMEM(occ_irreps.shape, jnp.int32),
            pltpu.SMEM(pair_list.shape[::-1], jnp.int32),
            dma((6,)),
            pltpu.VMEM((n_cols, height, LANES), jnp.bfloat16),
            pltpu.VMEM((n_rows, height, LANES), jnp.bfloat16),
            pltpu.VMEM((height, LANES), jnp.bfloat16),
            pltpu.VMEM((n_pairs, slab * width, width), jnp.bfloat16),
            pltpu.VMEM((n_pairs * slab * n_b, width * span), jnp.bfloat16),
            pltpu.VMEM((2, 2 * GROUP * height, span), jnp.float32),
            pltpu.VMEM((4 * n_a, width * span), jnp.bfloat16),
            pltpu.VMEM((n_pairs, slab * n_b, 2 * n_a), jnp.float32),
            pltpu.VMEM((n_pairs, slab * n_b, 2 * n_a), jnp.float32),
            dma((n_groups * (GROUP - 1),)), dma((n_cols // 2,)), dma((n_groups + 3,)), dma((n_cols,)),
            dma((n_x - 1,)), dma, dma((n_x,)), dma, dma((n_rows,)),
            dma((n_pairs,)), dma((n_pairs,)), dma((n_pairs,)), dma((n_pairs,)), dma((2,)),
            pltpu.SemaphoreType.REGULAR,
        ],
        compiler_params=pltpu.CompilerParams(
            collective_id=0, has_side_effects=True, vmem_limit_bytes=56 * 1024 * 1024
        ),
        name="ladder",
    )(jnp.transpose(factors, (1, 2, 0)), amplitudes, virt_irreps, win_irreps, occ_irreps, pair_list.T)
    return jnp.transpose(out.reshape(slab, n_rows, per_device, n_a), (0, 3, 1, 2))


def solution(mesh):
    in_specs = (P("pair", ("row", "col"), None), P("pair", None, None), P(), P(), P(), P())
    out_specs = P("pair", "row", None, "col")
    return jax.shard_map(body, mesh=mesh, in_specs=in_specs, out_specs=out_specs, check_vma=False)
```

```python
import functools

import jax
import jax.numpy as jnp
from jax import lax
from jax.experimental import pallas as pl
from jax.experimental.pallas import tpu as pltpu
from jax.sharding import PartitionSpec as P

MESH = pl.DeviceIdType.MESH
LANES = 512
GROUP = 4


def kernel(
    dims, x_hbm, amp_hbm, virt_hbm, win_hbm, occ_hbm, pairs_hbm, out_ref,
    x_ref, amp_ref, virt_ref, win_ref, occ_ref, pairs_ref, local,
    a_buf, b_buf, transit, w_buf, wide, integral, parts, sums, inbox,
    near_send, mate_send, chain_send, a_recv, side_send, cross_send, fan_send, cross_recv, b_recv,
    w_send, w_recv, r_send, r_recv, edge_send, ready,
):
    n_rows, n_cols, n_pairs, slab = dims
    row, col, pair = lax.axis_index("row"), lax.axis_index("col"), lax.axis_index("pair")
    width = amp_ref.shape[2]
    height = 2 * width
    n_fit = x_ref.shape[2]
    n_groups = n_cols // 2 // GROUP
    n_x = n_rows // 2
    core = lax.rem(col, 2)
    place = lax.rem(lax.div(col, 2), GROUP)
    group = lax.div(lax.div(col, 2), GROUP)
    upper = jnp.bitwise_and(row, 1) == 1

    def column(g, p):
        return (g * GROUP + p) * 2 + core

    def at(r=None, c=None, p=None):
        return (row if r is None else r, col if c is None else c, pair if p is None else p)

    near = [column(group, jnp.bitwise_xor(place, j)) for j in range(1, GROUP)]
    beside = near[0]
    mate = jnp.bitwise_xor(col, 1)
    half = jnp.bitwise_xor(row, 1)
    sides = [jnp.bitwise_xor(row, 2 * k) for k in range(1, n_x)]
    others = [jnp.bitwise_xor(pair, k) for k in range(1, n_pairs)]
    left, right = column(group - 1, place), column(group + 1, place)
    has_left, has_right = group > 0, group < n_groups - 1
    lower = jnp.logical_not(upper)
    at_first, at_last = jnp.logical_not(has_left), jnp.logical_not(has_right)
    direct_out = jnp.logical_and(upper, has_right)
    direct_in = jnp.logical_and(lower, has_right)
    edge = jnp.logical_or(at_first, at_last)
    low_edge, high_edge = jnp.logical_and(lower, edge), jnp.logical_and(upper, edge)
    leap = jnp.logical_and(lower, group >= 2)
    passes_left = jnp.logical_and(has_left, jnp.logical_or(upper, group >= 2))
    opposite = column(n_groups - 1 - group, place)
    inner = jnp.where(at_first, column(n_groups - 2, place), column(1, place))
    middle = jnp.logical_and(upper, jnp.logical_not(edge))
    outer = jnp.where(group == 1, column(n_groups - 1, place), column(0, place))

    barrier = pltpu.get_barrier_semaphore()

    def greet(peer):
        pl.semaphore_signal(barrier, inc=1, device_id=peer, device_id_type=MESH)

    peers = [at(c=c) for c in near + [mate]] + [at(r=r) for r in sides] + [at(p=p) for p in others]
    peers += [at(r=r, c=beside) for r in sides]
    for peer in peers:
        greet(peer)
    pl.when(has_right)(lambda: greet(at(c=right)))
    pl.when(jnp.logical_and(upper, has_left))(lambda: greet(at(c=left)))
    for g in range(2, n_groups):
        pl.when(jnp.logical_and(lower, at_first))(functools.partial(greet, at(c=column(g, place))))
    pl.when(low_edge)(lambda: greet(at(r=half, c=opposite)))
    pl.when(low_edge)(lambda: greet(at(r=half, c=inner)))
    pl.when(direct_in)(lambda: greet(at(r=half, c=beside)))

    loads = []
    operands = (
        (x_hbm, x_ref), (amp_hbm, amp_ref), (win_hbm, win_ref), (occ_hbm, occ_ref), (pairs_hbm, pairs_ref),
        (virt_hbm, virt_ref),
    )
    for i, (src, dst) in enumerate(operands):
        loads.append(pltpu.make_async_copy(src, dst, local.at[i]))
        loads[i].start()

    loads[0].wait()
    own = jnp.concatenate([x_ref[0], x_ref[1]], axis=0)
    own = jnp.concatenate([own, jnp.zeros((height, LANES - n_fit), own.dtype)], axis=1)
    a_buf[col] = own
    b_buf[row] = own

    awaited = len(peers) + jnp.where(has_left, 1, 0) + jnp.where(direct_out, 2, 0) + jnp.where(upper, 1, 0)
    awaited = awaited + jnp.where(leap, 1, 0)
    pl.semaphore_wait(barrier, awaited)
    pl.when(high_edge)(
        lambda: pl.semaphore_signal(ready.at[1], inc=1, device_id=at(r=half, c=opposite), device_id_type=MESH)
    )
    pl.when(middle)(
        lambda: pl.semaphore_signal(ready.at[0], inc=1, device_id=at(r=half, c=outer), device_id_type=MESH)
    )

    def copy(src, dst, sent, landed, target):
        return pltpu.make_async_remote_copy(
            src_ref=src, dst_ref=dst, send_sem=sent, recv_sem=landed, device_id=target, device_id_type=MESH
        )

    def block(slot, sent, c):
        return copy(a_buf.at[slot], a_buf.at[slot], sent, a_recv.at[slot], at(c=c))

    def cross():
        return copy(a_buf.at[col], transit, cross_send, cross_recv, at(r=half, c=beside))

    def fan(i, r):
        return copy(transit, b_buf.at[half], fan_send.at[i], b_recv.at[half], at(r=r, c=beside))

    def over(source, index):
        return copy(
            a_buf.at[source], b_buf.at[row], edge_send.at[index], b_recv.at[row],
            at(r=half, c=opposite if index else inner),
        )

    def share(i, r):
        return copy(b_buf.at[half], b_buf.at[half], fan_send.at[i + 1], b_recv.at[half], at(r=r))

    def side(i, r):
        return copy(b_buf.at[row], b_buf.at[row], side_send.at[i], b_recv.at[row], at(r=r))

    def near_copy(g, slot, j):
        return block(slot, near_send.at[g * (GROUP - 1) + j], near[j])

    def mate_copy(slot):
        return block(slot, mate_send.at[lax.div(slot, 2)], mate)

    def spread_block(g):
        slot = column(g, place)
        for j in range(GROUP - 1):
            near_copy(g, slot, j).start()
        mate_copy(slot).start()

    def chain(g, target, index):
        return block(column(g, place), chain_send.at[index], target)

    pl.when(direct_out)(lambda: cross().start())
    pl.when(leap)(lambda: chain(group, column(0, place), n_groups + 2).start())
    pl.when(has_left)(lambda: chain(group, left, n_groups).start())
    pl.when(jnp.logical_and(upper, has_right))(lambda: chain(group, right, n_groups + 1).start())
    spread_block(group)
    for i, r in enumerate(sides):
        side(i, r).start()

    for load in loads[1:]:
        load.wait()
    symmetry = []
    for s in range(slab):
        first, second = pairs_ref[0, pair * slab + s], pairs_ref[1, pair * slab + s]
        symmetry.append(jnp.bitwise_xor(occ_ref[first], occ_ref[second]))
    down = lax.broadcasted_iota(jnp.int32, (width, width), 0)
    across = lax.broadcasted_iota(jnp.int32, (width, width), 1)
    product = jnp.zeros((width, width), jnp.int32)
    for j in range(width):
        label = win_ref[j]
        product = jnp.bitwise_xor(product, jnp.where(down == j, label, 0))
        product = jnp.bitwise_xor(product, jnp.where(across == j, label, 0))
    for s in range(slab):
        kept = jnp.where(product == symmetry[s], amp_ref[s].astype(jnp.float32), 0.0)
        w_buf[pair, s * width:(s + 1) * width, :] = kept.astype(jnp.bfloat16)

    def give_weights(i):
        return copy(w_buf.at[pair], w_buf.at[pair], w_send.at[i], w_recv.at[pair], at(p=others[i]))

    for i in range(len(others)):
        give_weights(i).start()

    n_b = n_x * 2
    span = n_b * width
    tall = slab * n_b
    line = lax.broadcasted_iota(jnp.int32, (2 * n_b, span), 0)
    lane = lax.broadcasted_iota(jnp.int32, (2 * n_b, span), 1)
    own_b = lax.div(lane, width) == lax.rem(line, n_b)
    spread = (
        lax.rem(lax.broadcasted_iota(jnp.int32, (width, span), 1), width)
        == lax.broadcasted_iota(jnp.int32, (width, span), 0)
    ).astype(jnp.bfloat16)

    def expand(p):
        def one(s, carry):
            lines = jnp.dot(
                w_buf[p, pl.ds(pl.multiple_of(s * 2 * width, 2 * width), 2 * width), :], spread,
                preferred_element_type=jnp.float32,
            )
            start = pl.multiple_of(p * tall + s * 2 * n_b, 2 * n_b)
            for c in range(width):
                first = jnp.broadcast_to(lines[c:c + 1, :], own_b.shape)
                second = jnp.broadcast_to(lines[width + c:width + c + 1, :], own_b.shape)
                tile = jnp.where(own_b, jnp.where(line < n_b, first, second), 0.0)
                wide[pl.ds(start, 2 * n_b), c * span:(c + 1) * span] = tile.astype(jnp.bfloat16)
            return carry

        lax.fori_loop(0, slab // 2, one, 0)

    expand(pair)

    def onward():
        for d in range(n_groups - 2, n_groups):
            g = jnp.where(at_first, group + d, group - d)
            pl.semaphore_wait(ready.at[d - (n_groups - 2)], 1)
            over(column(g, place), d - (n_groups - 2)).start()

    def from_right(d):
        g = group + d
        block(column(g, place), chain_send.at[0], right).wait_recv()
        if d == 1:
            pl.when(lower)(lambda: chain(group, right, n_groups + 1).start())
        pl.when(passes_left)(lambda: chain(g, left, g).start())
        if d == n_groups - 1:
            pl.when(jnp.logical_and(upper, at_first))(lambda: over(column(g, place), 1).start())
        spread_block(g)

    def from_left(d):
        g = group - d
        block(column(g, place), chain_send.at[0], left).wait_recv()
        pl.when(has_right)(lambda: chain(g, right, g).start())
        spread_block(g)

    for d in range(1, n_groups):
        pl.when(group + d < n_groups)(functools.partial(from_right, d))
        pl.when(group - d >= 0)(functools.partial(from_left, d))
        if d == 1:
            for p in others:
                copy(w_buf.at[p], w_buf.at[p], w_send.at[0], w_recv.at[p], at(p=p)).wait_recv()
                expand(p)

    def handover(k, j):
        slot = column(jnp.bitwise_xor(group, k), jnp.bitwise_xor(place, j))
        block(slot, near_send.at[0], near[j - 1]).wait_recv()
        mate_copy(slot).start()

    def from_direct():
        cross().wait_recv()
        for i, r in enumerate([row] + sides):
            fan(i, r).start()

    def from_chain():
        share(0, row).wait_recv()
        for i, r in enumerate(sides):
            share(i, r).start()

    pl.when(low_edge)(onward)
    pl.when(upper)(from_chain)
    pl.when(direct_in)(from_direct)
    for k in range(n_groups):
        for j in range(1, GROUP):
            handover(k, j)
    pl.when(jnp.logical_and(lower, at_last))(from_chain)
    for r in sides:
        copy(b_buf.at[r], b_buf.at[r], side_send.at[0], b_recv.at[r], at(r=r)).wait_recv()
    here = jnp.bitwise_and(row, 1)
    n_a = 2 * n_cols
    label_lane = lax.broadcasted_iota(jnp.int32, (n_b, 2 * n_a), 1)
    label_line = lax.broadcasted_iota(jnp.int32, (n_b, 2 * n_a), 0)
    label = jnp.zeros((n_b, 2 * n_a), jnp.int32)
    lane_a = lax.rem(label_lane, n_a)
    for j in range(n_a):
        label = jnp.where(lane_a == j, virt_ref[row * n_a + j], label)
    for x in range(n_x):
        for m in range(2):
            mine = virt_ref[(2 * x + here) * n_a + col * 2 + m]
            far = virt_ref[(2 * x + 1 - here) * n_a + col * 2 + m]
            there = jnp.where(label_lane < n_a, mine, far)
            label = jnp.bitwise_xor(label, jnp.where(label_line == 2 * x + m, there, 0))

    def half_arrived(i):
        slot = jnp.bitwise_xor(half, 2 * i)
        copy(b_buf.at[slot], b_buf.at[slot], fan_send.at[0], b_recv.at[slot], at(r=half, c=beside)).wait_recv()

    pl.when(direct_in)(lambda: half_arrived(0))
    for i in range(1, n_x):
        half_arrived(i)
    b_rows = jnp.concatenate(
        [b_buf[2 * x + here] for x in range(n_x)] + [b_buf[2 * x + 1 - here] for x in range(n_x)], axis=0
    )
    b_rows = jnp.transpose(b_rows)
    deep = 2 * GROUP * height
    a_part = 2 * GROUP * 2

    def contract(k):
        g = jnp.bitwise_xor(group, k)
        for p in range(GROUP):
            slot = (g * GROUP + p) * 2 + 1 - core
            block(slot, mate_send.at[0], mate).wait_recv()
        rows = a_buf[pl.ds(pl.multiple_of(g * 2 * GROUP, 2 * GROUP), 2 * GROUP)].reshape(deep, LANES)
        tile = jnp.dot(rows, b_rows, preferred_element_type=jnp.float32)
        for t in range(2):
            integral[t] = tile[:, t * span:(t + 1) * span]
            start = pl.multiple_of(t * n_a + g * a_part, a_part)
            for c in range(width):
                lines = integral[t, pl.ds(c, a_part, stride=width), :]
                high = lines.astype(jnp.bfloat16)
                low = (lines - high.astype(jnp.float32)).astype(jnp.bfloat16)
                parts[pl.ds(start, a_part), c * span:(c + 1) * span] = high
                parts[pl.ds(pl.multiple_of(2 * n_a + start, a_part), a_part), c * span:(c + 1) * span] = low

    for k in range(n_groups):
        contract(k)

    def give_sum(i):
        return copy(sums.at[others[i]], inbox.at[pair], r_send.at[i], r_recv.at[pair], at(p=others[i]))

    both = lax.dot_general(wide[...], parts[...], (((1,), (1,)), ((), ())), preferred_element_type=jnp.float32)
    for p in range(n_pairs):
        sums[p] = both[p * tall:(p + 1) * tall, 0:2 * n_a] + both[p * tall:(p + 1) * tall, 2 * n_a:4 * n_a]
    for i in range(len(others)):
        give_sum(i).start()
    total = sums[pair]
    for p in others:
        copy(sums.at[p], inbox.at[p], r_send.at[0], r_recv.at[p], at(p=p)).wait_recv()
        total = total + inbox[p]
    for s in range(slab):
        kept = jnp.where(label == symmetry[s], total[s * n_b:(s + 1) * n_b], 0.0)
        mine, far = kept[:, 0:n_a], kept[:, n_a:2 * n_a]
        even, odd = jnp.where(upper, far, mine), jnp.where(upper, mine, far)
        for x in range(n_x):
            out_ref[s, 4 * x:4 * x + 2, :] = even[2 * x:2 * x + 2]
            out_ref[s, 4 * x + 2:4 * x + 4, :] = odd[2 * x:2 * x + 2]

    for g in range(n_groups):
        slot = column(g, place)
        for j in range(GROUP - 1):
            near_copy(g, slot, j).wait_send()
        pl.when(jnp.logical_or(jnp.logical_and(g > group, passes_left), jnp.logical_and(g < group, has_right)))(
            functools.partial(lambda g: chain(g, left, g).wait_send(), g)
        )
    pl.when(has_left)(lambda: chain(group, left, n_groups).wait_send())
    pl.when(leap)(lambda: chain(group, left, n_groups + 2).wait_send())
    pl.when(has_right)(lambda: chain(group, right, n_groups + 1).wait_send())
    for c in range(n_cols // 2):
        mate_copy(2 * c + core).wait_send()
    for i, r in enumerate(sides):
        side(i, r).wait_send()
    pl.when(direct_in)(lambda: fan(0, row).wait_send())
    for i, r in enumerate(sides):
        share(i, r).wait_send()
    pl.when(direct_out)(lambda: cross().wait_send())
    pl.when(low_edge)(lambda: over(col, 0).wait_send())
    pl.when(low_edge)(lambda: over(col, 1).wait_send())
    pl.when(jnp.logical_and(upper, at_first))(lambda: over(col, 1).wait_send())
    for i in range(len(others)):
        give_weights(i).wait_send()
        give_sum(i).wait_send()


def body(factors, amplitudes, virt_irreps, win_irreps, occ_irreps, pair_list):
    n_rows, n_cols, n_pairs = (lax.axis_size(name) for name in ("row", "col", "pair"))
    slab, width = amplitudes.shape[0], amplitudes.shape[1]
    per_device = factors.shape[1]
    n_a = per_device * n_cols
    n_x = n_rows // 2
    n_b = n_x * per_device
    span = n_b * width
    n_groups = n_cols // 2 // GROUP
    height = per_device * width
    hbm = pl.BlockSpec(memory_space=pltpu.HBM)
    dma = pltpu.SemaphoreType.DMA
    out = pl.pallas_call(
        functools.partial(kernel, (n_rows, n_cols, n_pairs, slab)),
        out_shape=jax.ShapeDtypeStruct((slab, n_rows * per_device, n_a), jnp.float32),
        in_specs=[hbm] * 6,
        out_specs=pl.BlockSpec(memory_space=pltpu.VMEM),
        scratch_shapes=[
            pltpu.VMEM((per_device, width, factors.shape[0]), factors.dtype),
            pltpu.VMEM(amplitudes.shape, amplitudes.dtype),
            pltpu.SMEM(virt_irreps.shape, jnp.int32),
            pltpu.SMEM(win_irreps.shape, jnp.int32),
            pltpu.SMEM(occ_irreps.shape, jnp.int32),
            pltpu.SMEM(pair_list.shape[::-1], jnp.int32),
            dma((6,)),
            pltpu.VMEM((n_cols, height, LANES), jnp.bfloat16),
            pltpu.VMEM((n_rows, height, LANES), jnp.bfloat16),
            pltpu.VMEM((height, LANES), jnp.bfloat16),
            pltpu.VMEM((n_pairs, slab * width, width), jnp.bfloat16),
            pltpu.VMEM((n_pairs * slab * n_b, width * span), jnp.bfloat16),
            pltpu.VMEM((2, 2 * GROUP * height, span), jnp.float32),
            pltpu.VMEM((4 * n_a, width * span), jnp.bfloat16),
            pltpu.VMEM((n_pairs, slab * n_b, 2 * n_a), jnp.float32),
            pltpu.VMEM((n_pairs, slab * n_b, 2 * n_a), jnp.float32),
            dma((n_groups * (GROUP - 1),)), dma((n_cols // 2,)), dma((n_groups + 3,)), dma((n_cols,)),
            dma((n_x - 1,)), dma, dma((n_x,)), dma, dma((n_rows,)),
            dma((n_pairs,)), dma((n_pairs,)), dma((n_pairs,)), dma((n_pairs,)), dma((2,)),
            pltpu.SemaphoreType.REGULAR((2,)),
        ],
        compiler_params=pltpu.CompilerParams(
            collective_id=0, has_side_effects=True, vmem_limit_bytes=56 * 1024 * 1024
        ),
        name="ladder",
    )(jnp.transpose(factors, (1, 2, 0)), amplitudes, virt_irreps, win_irreps, occ_irreps, pair_list.T)
    return jnp.transpose(out.reshape(slab, n_rows, per_device, n_a), (0, 3, 1, 2))


def solution(mesh):
    in_specs = (P("pair", ("row", "col"), None), P("pair", None, None), P(), P(), P(), P())
    out_specs = P("pair", "row", None, "col")
    return jax.shard_map(body, mesh=mesh, in_specs=in_specs, out_specs=out_specs, check_vma=False)
```

```python
import functools

import jax
import jax.numpy as jnp
from jax import lax
from jax.experimental import pallas as pl
from jax.experimental.pallas import tpu as pltpu
from jax.sharding import PartitionSpec as P

MESH = pl.DeviceIdType.MESH
LANES = 512
GROUP = 4


def kernel(
    dims, x_hbm, amp_hbm, virt_hbm, win_hbm, occ_hbm, pairs_hbm, out_ref,
    x_ref, amp_ref, virt_ref, win_ref, occ_ref, pairs_ref, local,
    a_buf, b_buf, transit, w_buf, wide, integral, parts, sums, inbox,
    near_send, mate_send, chain_send, a_recv, side_send, cross_send, fan_send, cross_recv, b_recv,
    w_send, w_recv, r_send, r_recv, edge_send, ready,
):
    n_rows, n_cols, n_pairs, slab = dims
    row, col, pair = lax.axis_index("row"), lax.axis_index("col"), lax.axis_index("pair")
    width = amp_ref.shape[2]
    height = 2 * width
    n_fit = x_ref.shape[2]
    n_groups = n_cols // 2 // GROUP
    n_x = n_rows // 2
    core = lax.rem(col, 2)
    place = lax.rem(lax.div(col, 2), GROUP)
    group = lax.div(lax.div(col, 2), GROUP)
    upper = jnp.bitwise_and(row, 1) == 1

    def column(g, p):
        return (g * GROUP + p) * 2 + core

    def at(r=None, c=None, p=None):
        return (row if r is None else r, col if c is None else c, pair if p is None else p)

    near = [column(group, jnp.bitwise_xor(place, j)) for j in range(1, GROUP)]
    beside = near[0]
    mate = jnp.bitwise_xor(col, 1)
    half = jnp.bitwise_xor(row, 1)
    sides = [jnp.bitwise_xor(row, 2 * k) for k in range(1, n_x)]
    others = [jnp.bitwise_xor(pair, k) for k in range(1, n_pairs)]
    left, right = column(group - 1, place), column(group + 1, place)
    has_left, has_right = group > 0, group < n_groups - 1
    lower = jnp.logical_not(upper)
    at_first, at_last = jnp.logical_not(has_left), jnp.logical_not(has_right)
    direct_out = jnp.logical_and(upper, has_right)
    direct_in = jnp.logical_and(lower, has_right)
    edge = jnp.logical_or(at_first, at_last)
    low_edge, high_edge = jnp.logical_and(lower, edge), jnp.logical_and(upper, edge)
    leap = jnp.logical_and(lower, group >= 2)
    passes_left = jnp.logical_and(has_left, jnp.logical_or(upper, group >= 2))
    opposite = column(n_groups - 1 - group, place)
    inner = jnp.where(at_first, column(n_groups - 2, place), column(1, place))
    middle = jnp.logical_and(upper, jnp.logical_not(edge))
    outer = jnp.where(group == 1, column(n_groups - 1, place), column(0, place))

    barrier = pltpu.get_barrier_semaphore()

    def greet(peer):
        pl.semaphore_signal(barrier, inc=1, device_id=peer, device_id_type=MESH)

    peers = [at(c=c) for c in near + [mate]] + [at(r=r) for r in sides] + [at(p=p) for p in others]
    peers += [at(r=r, c=beside) for r in sides]
    for peer in peers:
        greet(peer)
    pl.when(has_right)(lambda: greet(at(c=right)))
    pl.when(jnp.logical_and(upper, has_left))(lambda: greet(at(c=left)))
    for g in range(2, n_groups):
        pl.when(jnp.logical_and(lower, at_first))(functools.partial(greet, at(c=column(g, place))))
    pl.when(low_edge)(lambda: greet(at(r=half, c=opposite)))
    pl.when(low_edge)(lambda: greet(at(r=half, c=inner)))
    pl.when(direct_in)(lambda: greet(at(r=half, c=beside)))

    loads = []
    operands = (
        (x_hbm, x_ref), (amp_hbm, amp_ref), (win_hbm, win_ref), (occ_hbm, occ_ref), (pairs_hbm, pairs_ref),
        (virt_hbm, virt_ref),
    )
    for i, (src, dst) in enumerate(operands):
        loads.append(pltpu.make_async_copy(src, dst, local.at[i]))
        loads[i].start()

    loads[0].wait()
    own = jnp.concatenate([x_ref[0], x_ref[1]], axis=0)
    own = jnp.concatenate([own, jnp.zeros((height, LANES - n_fit), own.dtype)], axis=1)
    a_buf[col] = own
    b_buf[row] = own

    awaited = len(peers) + jnp.where(has_left, 1, 0) + jnp.where(direct_out, 2, 0) + jnp.where(upper, 1, 0)
    awaited = awaited + jnp.where(leap, 1, 0)
    pl.semaphore_wait(barrier, awaited)
    pl.when(high_edge)(
        lambda: pl.semaphore_signal(ready.at[1], inc=1, device_id=at(r=half, c=opposite), device_id_type=MESH)
    )
    pl.when(middle)(
        lambda: pl.semaphore_signal(ready.at[0], inc=1, device_id=at(r=half, c=outer), device_id_type=MESH)
    )

    def copy(src, dst, sent, landed, target):
        return pltpu.make_async_remote_copy(
            src_ref=src, dst_ref=dst, send_sem=sent, recv_sem=landed, device_id=target, device_id_type=MESH
        )

    def block(slot, sent, c):
        return copy(a_buf.at[slot], a_buf.at[slot], sent, a_recv.at[slot], at(c=c))

    def cross():
        return copy(a_buf.at[col], transit, cross_send, cross_recv, at(r=half, c=beside))

    def fan(i, r):
        return copy(transit, b_buf.at[half], fan_send.at[i], b_recv.at[half], at(r=r, c=beside))

    def over(source, index):
        return copy(
            a_buf.at[source], b_buf.at[row], edge_send.at[index], b_recv.at[row],
            at(r=half, c=opposite if index else inner),
        )

    def share(i, r):
        return copy(b_buf.at[half], b_buf.at[half], fan_send.at[i + 1], b_recv.at[half], at(r=r))

    def side(i, r):
        return copy(b_buf.at[row], b_buf.at[row], side_send.at[i], b_recv.at[row], at(r=r))

    def near_copy(g, slot, j):
        return block(slot, near_send.at[g * (GROUP - 1) + j], near[j])

    def mate_copy(slot):
        return block(slot, mate_send.at[lax.div(slot, 2)], mate)

    def spread_block(g):
        slot = column(g, place)
        for j in range(GROUP - 1):
            near_copy(g, slot, j).start()
        mate_copy(slot).start()

    def chain(g, target, index):
        return block(column(g, place), chain_send.at[index], target)

    pl.when(direct_out)(lambda: cross().start())
    pl.when(leap)(lambda: chain(group, column(0, place), n_groups + 2).start())
    pl.when(has_left)(lambda: chain(group, left, n_groups).start())
    pl.when(jnp.logical_and(upper, has_right))(lambda: chain(group, right, n_groups + 1).start())
    spread_block(group)
    for i, r in enumerate(sides):
        side(i, r).start()

    for load in loads[1:]:
        load.wait()
    symmetry = []
    for s in range(slab):
        first, second = pairs_ref[0, pair * slab + s], pairs_ref[1, pair * slab + s]
        symmetry.append(jnp.bitwise_xor(occ_ref[first], occ_ref[second]))
    down = lax.broadcasted_iota(jnp.int32, (width, width), 0)
    across = lax.broadcasted_iota(jnp.int32, (width, width), 1)
    product = jnp.zeros((width, width), jnp.int32)
    for j in range(width):
        label = win_ref[j]
        product = jnp.bitwise_xor(product, jnp.where(down == j, label, 0))
        product = jnp.bitwise_xor(product, jnp.where(across == j, label, 0))
    for s in range(slab):
        kept = jnp.where(product == symmetry[s], amp_ref[s].astype(jnp.float32), 0.0)
        w_buf[pair, s * width:(s + 1) * width, :] = kept.astype(jnp.bfloat16)

    def give_weights(i):
        return copy(w_buf.at[pair], w_buf.at[pair], w_send.at[i], w_recv.at[pair], at(p=others[i]))

    for i in range(len(others)):
        give_weights(i).start()

    n_b = n_x * 2
    span = n_b * width
    tall = slab * n_b
    line = lax.broadcasted_iota(jnp.int32, (2 * n_b, span), 0)
    lane = lax.broadcasted_iota(jnp.int32, (2 * n_b, span), 1)
    own_b = lax.div(lane, width) == lax.rem(line, n_b)
    spread = (
        lax.rem(lax.broadcasted_iota(jnp.int32, (width, span), 1), width)
        == lax.broadcasted_iota(jnp.int32, (width, span), 0)
    ).astype(jnp.bfloat16)

    def expand(p):
        def one(s, carry):
            lines = jnp.dot(
                w_buf[p, pl.ds(pl.multiple_of(s * 2 * width, 2 * width), 2 * width), :], spread,
                preferred_element_type=jnp.float32,
            )
            start = pl.multiple_of(p * tall + s * 2 * n_b, 2 * n_b)
            for c in range(width):
                first = jnp.broadcast_to(lines[c:c + 1, :], own_b.shape)
                second = jnp.broadcast_to(lines[width + c:width + c + 1, :], own_b.shape)
                tile = jnp.where(own_b, jnp.where(line < n_b, first, second), 0.0)
                wide[pl.ds(start, 2 * n_b), c * span:(c + 1) * span] = tile.astype(jnp.bfloat16)
            return carry

        lax.fori_loop(0, slab // 2, one, 0)

    expand(pair)

    def onward(d, g):
        pl.semaphore_wait(ready.at[d - (n_groups - 2)], 1)
        over(column(g, place), d - (n_groups - 2)).start()

    def from_right(d):
        g = group + d
        block(column(g, place), chain_send.at[0], right).wait_recv()
        if d == 1:
            pl.when(lower)(lambda: chain(group, right, n_groups + 1).start())
        pl.when(passes_left)(lambda: chain(g, left, g).start())
        if d == n_groups - 1:
            pl.when(jnp.logical_and(upper, at_first))(lambda: over(column(g, place), 1).start())
        spread_block(g)

    def from_left(d):
        g = group - d
        block(column(g, place), chain_send.at[0], left).wait_recv()
        pl.when(has_right)(lambda: chain(g, right, g).start())
        spread_block(g)
        if d >= n_groups - 2:
            pl.when(jnp.logical_and(at_last, lower))(lambda: onward(d, g))

    for d in range(1, n_groups):
        pl.when(group + d < n_groups)(functools.partial(from_right, d))
        pl.when(group - d >= 0)(functools.partial(from_left, d))
        if d == 1:
            for p in others:
                copy(w_buf.at[p], w_buf.at[p], w_send.at[0], w_recv.at[p], at(p=p)).wait_recv()
                expand(p)

    def handover(k, j):
        slot = column(jnp.bitwise_xor(group, k), jnp.bitwise_xor(place, j))
        block(slot, near_send.at[0], near[j - 1]).wait_recv()
        mate_copy(slot).start()

    def from_direct():
        cross().wait_recv()
        for i, r in enumerate([row] + sides):
            fan(i, r).start()

    def from_chain():
        share(0, row).wait_recv()
        for i, r in enumerate(sides):
            share(i, r).start()

    for d in range(n_groups - 2, n_groups):
        pl.when(jnp.logical_and(at_first, lower))(functools.partial(onward, d, group + d))
    pl.when(upper)(from_chain)
    pl.when(direct_in)(from_direct)
    for k in range(n_groups):
        for j in range(1, GROUP):
            handover(k, j)
    pl.when(jnp.logical_and(lower, at_last))(from_chain)
    for r in sides:
        copy(b_buf.at[r], b_buf.at[r], side_send.at[0], b_recv.at[r], at(r=r)).wait_recv()
    here = jnp.bitwise_and(row, 1)
    n_a = 2 * n_cols
    label_lane = lax.broadcasted_iota(jnp.int32, (n_b, 2 * n_a), 1)
    label_line = lax.broadcasted_iota(jnp.int32, (n_b, 2 * n_a), 0)
    label = jnp.zeros((n_b, 2 * n_a), jnp.int32)
    lane_a = lax.rem(label_lane, n_a)
    for j in range(n_a):
        label = jnp.where(lane_a == j, virt_ref[row * n_a + j], label)
    for x in range(n_x):
        for m in range(2):
            mine = virt_ref[(2 * x + here) * n_a + col * 2 + m]
            far = virt_ref[(2 * x + 1 - here) * n_a + col * 2 + m]
            there = jnp.where(label_lane < n_a, mine, far)
            label = jnp.bitwise_xor(label, jnp.where(label_line == 2 * x + m, there, 0))

    def half_arrived(i):
        slot = jnp.bitwise_xor(half, 2 * i)
        copy(b_buf.at[slot], b_buf.at[slot], fan_send.at[0], b_recv.at[slot], at(r=half, c=beside)).wait_recv()

    def b_side(h):
        return jnp.transpose(jnp.concatenate([b_buf[2 * x + h] for x in range(n_x)], axis=0))

    deep = 2 * GROUP * height
    a_part = 2 * GROUP * 2

    def contract(k, t, b_rows):
        g = jnp.bitwise_xor(group, k)
        rows = a_buf[pl.ds(pl.multiple_of(g * 2 * GROUP, 2 * GROUP), 2 * GROUP)].reshape(deep, LANES)
        integral[t] = jnp.dot(rows, b_rows, preferred_element_type=jnp.float32)
        start = pl.multiple_of(t * n_a + g * a_part, a_part)
        for c in range(width):
            lines = integral[t, pl.ds(c, a_part, stride=width), :]
            high = lines.astype(jnp.bfloat16)
            low = (lines - high.astype(jnp.float32)).astype(jnp.bfloat16)
            parts[pl.ds(start, a_part), c * span:(c + 1) * span] = high
            parts[pl.ds(pl.multiple_of(2 * n_a + start, a_part), a_part), c * span:(c + 1) * span] = low

    b_near = b_side(here)
    for k in range(n_groups):
        for p in range(GROUP):
            slot = (jnp.bitwise_xor(group, k) * GROUP + p) * 2 + 1 - core
            block(slot, mate_send.at[0], mate).wait_recv()
        contract(k, 0, b_near)
    pl.when(direct_in)(lambda: half_arrived(0))
    for i in range(1, n_x):
        half_arrived(i)
    b_far = b_side(1 - here)
    for k in range(n_groups):
        contract(k, 1, b_far)

    def give_sum(i):
        return copy(sums.at[others[i]], inbox.at[pair], r_send.at[i], r_recv.at[pair], at(p=others[i]))

    both = lax.dot_general(wide[...], parts[...], (((1,), (1,)), ((), ())), preferred_element_type=jnp.float32)
    for p in range(n_pairs):
        sums[p] = both[p * tall:(p + 1) * tall, 0:2 * n_a] + both[p * tall:(p + 1) * tall, 2 * n_a:4 * n_a]
    for i in range(len(others)):
        give_sum(i).start()
    total = sums[pair]
    for p in others:
        copy(sums.at[p], inbox.at[p], r_send.at[0], r_recv.at[p], at(p=p)).wait_recv()
        total = total + inbox[p]
    for s in range(slab):
        kept = jnp.where(label == symmetry[s], total[s * n_b:(s + 1) * n_b], 0.0)
        mine, far = kept[:, 0:n_a], kept[:, n_a:2 * n_a]
        even, odd = jnp.where(upper, far, mine), jnp.where(upper, mine, far)
        for x in range(n_x):
            out_ref[s, 4 * x:4 * x + 2, :] = even[2 * x:2 * x + 2]
            out_ref[s, 4 * x + 2:4 * x + 4, :] = odd[2 * x:2 * x + 2]

    for g in range(n_groups):
        slot = column(g, place)
        for j in range(GROUP - 1):
            near_copy(g, slot, j).wait_send()
        pl.when(jnp.logical_or(jnp.logical_and(g > group, passes_left), jnp.logical_and(g < group, has_right)))(
            functools.partial(lambda g: chain(g, left, g).wait_send(), g)
        )
    pl.when(has_left)(lambda: chain(group, left, n_groups).wait_send())
    pl.when(leap)(lambda: chain(group, left, n_groups + 2).wait_send())
    pl.when(has_right)(lambda: chain(group, right, n_groups + 1).wait_send())
    for c in range(n_cols // 2):
        mate_copy(2 * c + core).wait_send()
    for i, r in enumerate(sides):
        side(i, r).wait_send()
    pl.when(direct_in)(lambda: fan(0, row).wait_send())
    for i, r in enumerate(sides):
        share(i, r).wait_send()
    pl.when(direct_out)(lambda: cross().wait_send())
    pl.when(low_edge)(lambda: over(col, 0).wait_send())
    pl.when(low_edge)(lambda: over(col, 1).wait_send())
    pl.when(jnp.logical_and(upper, at_first))(lambda: over(col, 1).wait_send())
    for i in range(len(others)):
        give_weights(i).wait_send()
        give_sum(i).wait_send()


def body(factors, amplitudes, virt_irreps, win_irreps, occ_irreps, pair_list):
    n_rows, n_cols, n_pairs = (lax.axis_size(name) for name in ("row", "col", "pair"))
    slab, width = amplitudes.shape[0], amplitudes.shape[1]
    per_device = factors.shape[1]
    n_a = per_device * n_cols
    n_x = n_rows // 2
    n_b = n_x * per_device
    span = n_b * width
    n_groups = n_cols // 2 // GROUP
    height = per_device * width
    hbm = pl.BlockSpec(memory_space=pltpu.HBM)
    dma = pltpu.SemaphoreType.DMA
    out = pl.pallas_call(
        functools.partial(kernel, (n_rows, n_cols, n_pairs, slab)),
        out_shape=jax.ShapeDtypeStruct((slab, n_rows * per_device, n_a), jnp.float32),
        in_specs=[hbm] * 6,
        out_specs=pl.BlockSpec(memory_space=pltpu.VMEM),
        scratch_shapes=[
            pltpu.VMEM((per_device, width, factors.shape[0]), factors.dtype),
            pltpu.VMEM(amplitudes.shape, amplitudes.dtype),
            pltpu.SMEM(virt_irreps.shape, jnp.int32),
            pltpu.SMEM(win_irreps.shape, jnp.int32),
            pltpu.SMEM(occ_irreps.shape, jnp.int32),
            pltpu.SMEM(pair_list.shape[::-1], jnp.int32),
            dma((6,)),
            pltpu.VMEM((n_cols, height, LANES), jnp.bfloat16),
            pltpu.VMEM((n_rows, height, LANES), jnp.bfloat16),
            pltpu.VMEM((height, LANES), jnp.bfloat16),
            pltpu.VMEM((n_pairs, slab * width, width), jnp.bfloat16),
            pltpu.VMEM((n_pairs * slab * n_b, width * span), jnp.bfloat16),
            pltpu.VMEM((2, 2 * GROUP * height, span), jnp.float32),
            pltpu.VMEM((4 * n_a, width * span), jnp.bfloat16),
            pltpu.VMEM((n_pairs, slab * n_b, 2 * n_a), jnp.float32),
            pltpu.VMEM((n_pairs, slab * n_b, 2 * n_a), jnp.float32),
            dma((n_groups * (GROUP - 1),)), dma((n_cols // 2,)), dma((n_groups + 3,)), dma((n_cols,)),
            dma((n_x - 1,)), dma, dma((n_x,)), dma, dma((n_rows,)),
            dma((n_pairs,)), dma((n_pairs,)), dma((n_pairs,)), dma((n_pairs,)), dma((2,)),
            pltpu.SemaphoreType.REGULAR((2,)),
        ],
        compiler_params=pltpu.CompilerParams(
            collective_id=0, has_side_effects=True, vmem_limit_bytes=56 * 1024 * 1024
        ),
        name="ladder",
    )(jnp.transpose(factors, (1, 2, 0)), amplitudes, virt_irreps, win_irreps, occ_irreps, pair_list.T)
    return jnp.transpose(out.reshape(slab, n_rows, per_device, n_a), (0, 3, 1, 2))


def solution(mesh):
    in_specs = (P("pair", ("row", "col"), None), P("pair", None, None), P(), P(), P(), P())
    out_specs = P("pair", "row", None, "col")
    return jax.shard_map(body, mesh=mesh, in_specs=in_specs, out_specs=out_specs, check_vma=False)
```

```python
import functools

import jax
import jax.numpy as jnp
from jax import lax
from jax.experimental import pallas as pl
from jax.experimental.pallas import tpu as pltpu
from jax.sharding import PartitionSpec as P

MESH = pl.DeviceIdType.MESH
LANES = 512
GROUP = 4


def kernel(
    dims, x_hbm, amp_hbm, virt_hbm, win_hbm, occ_hbm, pairs_hbm, out_ref,
    x_ref, amp_ref, virt_ref, win_ref, occ_ref, pairs_ref, local,
    a_buf, b_buf, transit, w_buf, wide, integral, parts, sums, inbox,
    near_send, mate_send, chain_send, a_recv, side_send, cross_send, fan_send, cross_recv, b_recv,
    w_send, w_recv, r_send, r_recv, edge_send, ready,
):
    n_rows, n_cols, n_pairs, slab = dims
    row, col, pair = lax.axis_index("row"), lax.axis_index("col"), lax.axis_index("pair")
    width = amp_ref.shape[2]
    height = 2 * width
    n_fit = x_ref.shape[2]
    n_groups = n_cols // 2 // GROUP
    n_x = n_rows // 2
    core = lax.rem(col, 2)
    place = lax.rem(lax.div(col, 2), GROUP)
    group = lax.div(lax.div(col, 2), GROUP)
    upper = jnp.bitwise_and(row, 1) == 1

    def column(g, p):
        return (g * GROUP + p) * 2 + core

    def at(r=None, c=None, p=None):
        return (row if r is None else r, col if c is None else c, pair if p is None else p)

    near = [column(group, jnp.bitwise_xor(place, j)) for j in range(1, GROUP)]
    beside = jnp.bitwise_xor(near[0], jnp.where(place < 2, 0, 1))
    mate = jnp.bitwise_xor(col, 1)
    half = jnp.bitwise_xor(row, 1)
    sides = [jnp.bitwise_xor(row, 2 * k) for k in range(1, n_x)]
    others = [jnp.bitwise_xor(pair, k) for k in range(1, n_pairs)]
    left, right = column(group - 1, place), column(group + 1, place)
    has_left, has_right = group > 0, group < n_groups - 1
    lower = jnp.logical_not(upper)
    at_first, at_last = jnp.logical_not(has_left), jnp.logical_not(has_right)
    direct_out = jnp.logical_and(upper, has_right)
    direct_in = jnp.logical_and(lower, has_right)
    edge = jnp.logical_or(at_first, at_last)
    low_edge, high_edge = jnp.logical_and(lower, edge), jnp.logical_and(upper, edge)
    leap = jnp.logical_and(lower, group >= 2)
    passes_left = jnp.logical_and(has_left, jnp.logical_or(upper, group >= 2))
    opposite = column(n_groups - 1 - group, place)
    inner = jnp.where(at_first, column(n_groups - 2, place), column(1, place))
    middle = jnp.logical_and(upper, jnp.logical_not(edge))
    outer = jnp.where(group == 1, column(n_groups - 1, place), column(0, place))

    barrier = pltpu.get_barrier_semaphore()

    def greet(peer):
        pl.semaphore_signal(barrier, inc=1, device_id=peer, device_id_type=MESH)

    peers = [at(c=c) for c in near + [mate]] + [at(r=r) for r in sides] + [at(p=p) for p in others]
    peers += [at(r=r, c=beside) for r in [row] + sides]
    for peer in peers:
        greet(peer)
    pl.when(has_right)(lambda: greet(at(c=right)))
    pl.when(jnp.logical_and(upper, has_left))(lambda: greet(at(c=left)))
    for g in range(2, n_groups):
        pl.when(jnp.logical_and(lower, at_first))(functools.partial(greet, at(c=column(g, place))))
    pl.when(low_edge)(lambda: greet(at(r=half, c=opposite)))
    pl.when(low_edge)(lambda: greet(at(r=half, c=inner)))
    pl.when(direct_in)(lambda: greet(at(r=half, c=beside)))

    loads = []
    operands = (
        (x_hbm, x_ref), (amp_hbm, amp_ref), (win_hbm, win_ref), (occ_hbm, occ_ref), (pairs_hbm, pairs_ref),
        (virt_hbm, virt_ref),
    )
    for i, (src, dst) in enumerate(operands):
        loads.append(pltpu.make_async_copy(src, dst, local.at[i]))
        loads[i].start()

    loads[0].wait()
    own = jnp.concatenate([x_ref[0], x_ref[1]], axis=0)
    own = jnp.concatenate([own, jnp.zeros((height, LANES - n_fit), own.dtype)], axis=1)
    a_buf[col] = own
    b_buf[row] = own

    awaited = len(peers) + jnp.where(has_left, 1, 0) + jnp.where(direct_out, 2, 0) + jnp.where(upper, 1, 0)
    awaited = awaited + jnp.where(leap, 1, 0)
    pl.semaphore_wait(barrier, awaited)
    pl.when(high_edge)(
        lambda: pl.semaphore_signal(ready.at[1], inc=1, device_id=at(r=half, c=opposite), device_id_type=MESH)
    )
    pl.when(middle)(
        lambda: pl.semaphore_signal(ready.at[0], inc=1, device_id=at(r=half, c=outer), device_id_type=MESH)
    )

    def copy(src, dst, sent, landed, target):
        return pltpu.make_async_remote_copy(
            src_ref=src, dst_ref=dst, send_sem=sent, recv_sem=landed, device_id=target, device_id_type=MESH
        )

    def block(slot, sent, c):
        return copy(a_buf.at[slot], a_buf.at[slot], sent, a_recv.at[slot], at(c=c))

    def cross():
        return copy(a_buf.at[col], transit, cross_send, cross_recv, at(r=half, c=beside))

    def fan(i, r):
        return copy(transit, b_buf.at[half], fan_send.at[i], b_recv.at[half], at(r=r, c=beside))

    def over(source, index):
        return copy(
            a_buf.at[source], b_buf.at[row], edge_send.at[index], b_recv.at[row],
            at(r=half, c=opposite if index else inner),
        )

    def share(i, r):
        return copy(b_buf.at[half], b_buf.at[half], fan_send.at[i + 1], b_recv.at[half], at(r=r))

    def side(i, r):
        return copy(b_buf.at[row], b_buf.at[row], side_send.at[i], b_recv.at[row], at(r=r))

    def near_copy(g, slot, j):
        return block(slot, near_send.at[g * (GROUP - 1) + j], near[j])

    def mate_copy(slot):
        return block(slot, mate_send.at[lax.div(slot, 2)], mate)

    def spread_block(g):
        slot = column(g, place)
        for j in range(GROUP - 1):
            near_copy(g, slot, j).start()
        mate_copy(slot).start()

    def chain(g, target, index):
        return block(column(g, place), chain_send.at[index], target)

    pl.when(direct_out)(lambda: cross().start())
    pl.when(leap)(lambda: chain(group, column(0, place), n_groups + 2).start())
    pl.when(has_left)(lambda: chain(group, left, n_groups).start())
    pl.when(jnp.logical_and(upper, has_right))(lambda: chain(group, right, n_groups + 1).start())
    spread_block(group)
    for i, r in enumerate(sides):
        side(i, r).start()

    for load in loads[1:]:
        load.wait()
    symmetry = []
    for s in range(slab):
        first, second = pairs_ref[0, pair * slab + s], pairs_ref[1, pair * slab + s]
        symmetry.append(jnp.bitwise_xor(occ_ref[first], occ_ref[second]))
    down = lax.broadcasted_iota(jnp.int32, (width, width), 0)
    across = lax.broadcasted_iota(jnp.int32, (width, width), 1)
    product = jnp.zeros((width, width), jnp.int32)
    for j in range(width):
        label = win_ref[j]
        product = jnp.bitwise_xor(product, jnp.where(down == j, label, 0))
        product = jnp.bitwise_xor(product, jnp.where(across == j, label, 0))
    for s in range(slab):
        kept = jnp.where(product == symmetry[s], amp_ref[s].astype(jnp.float32), 0.0)
        w_buf[pair, s * width:(s + 1) * width, :] = kept.astype(jnp.bfloat16)

    def give_weights(i):
        return copy(w_buf.at[pair], w_buf.at[pair], w_send.at[i], w_recv.at[pair], at(p=others[i]))

    for i in range(len(others)):
        give_weights(i).start()

    n_b = n_x * 2
    here = jnp.bitwise_and(row, 1)
    n_a = 2 * n_cols
    label_lane = lax.broadcasted_iota(jnp.int32, (n_b, 2 * n_a), 1)
    label_line = lax.broadcasted_iota(jnp.int32, (n_b, 2 * n_a), 0)
    label = jnp.zeros((n_b, 2 * n_a), jnp.int32)
    lane_a = lax.rem(label_lane, n_a)
    for j in range(n_a):
        label = jnp.where(lane_a == j, virt_ref[row * n_a + j], label)
    for x in range(n_x):
        for m in range(2):
            mine = virt_ref[(2 * x + here) * n_a + col * 2 + m]
            far = virt_ref[(2 * x + 1 - here) * n_a + col * 2 + m]
            there = jnp.where(label_lane < n_a, mine, far)
            label = jnp.bitwise_xor(label, jnp.where(label_line == 2 * x + m, there, 0))

    span = n_b * width
    tall = slab * n_b
    line = lax.broadcasted_iota(jnp.int32, (2 * n_b, span), 0)
    lane = lax.broadcasted_iota(jnp.int32, (2 * n_b, span), 1)
    own_b = lax.div(lane, width) == lax.rem(line, n_b)
    spread = (
        lax.rem(lax.broadcasted_iota(jnp.int32, (width, span), 1), width)
        == lax.broadcasted_iota(jnp.int32, (width, span), 0)
    ).astype(jnp.bfloat16)

    def expand(p):
        def one(s, carry):
            lines = jnp.dot(
                w_buf[p, pl.ds(pl.multiple_of(s * 2 * width, 2 * width), 2 * width), :], spread,
                preferred_element_type=jnp.float32,
            )
            start = pl.multiple_of(p * tall + s * 2 * n_b, 2 * n_b)
            for c in range(width):
                first = jnp.broadcast_to(lines[c:c + 1, :], own_b.shape)
                second = jnp.broadcast_to(lines[width + c:width + c + 1, :], own_b.shape)
                tile = jnp.where(own_b, jnp.where(line < n_b, first, second), 0.0)
                wide[pl.ds(start, 2 * n_b), c * span:(c + 1) * span] = tile.astype(jnp.bfloat16)
            return carry

        lax.fori_loop(0, slab // 2, one, 0)

    expand(pair)

    def onward(d, g):
        pl.semaphore_wait(ready.at[d - (n_groups - 2)], 1)
        over(column(g, place), d - (n_groups - 2)).start()

    def from_right(d):
        g = group + d
        block(column(g, place), chain_send.at[0], right).wait_recv()
        if d == 1:
            pl.when(lower)(lambda: chain(group, right, n_groups + 1).start())
        pl.when(passes_left)(lambda: chain(g, left, g).start())
        if d == n_groups - 1:
            pl.when(jnp.logical_and(upper, at_first))(lambda: over(column(g, place), 1).start())
        spread_block(g)

    def from_left(d):
        g = group - d
        block(column(g, place), chain_send.at[0], left).wait_recv()
        pl.when(has_right)(lambda: chain(g, right, g).start())
        spread_block(g)
        if d >= n_groups - 2:
            pl.when(jnp.logical_and(at_last, lower))(lambda: onward(d, g))

    for d in range(1, n_groups):
        pl.when(group + d < n_groups)(functools.partial(from_right, d))
        pl.when(group - d >= 0)(functools.partial(from_left, d))
        if d == 1:
            for p in others:
                copy(w_buf.at[p], w_buf.at[p], w_send.at[0], w_recv.at[p], at(p=p)).wait_recv()
                expand(p)

    def handover(k, j):
        slot = column(jnp.bitwise_xor(group, k), jnp.bitwise_xor(place, j))
        block(slot, near_send.at[0], near[j - 1]).wait_recv()
        mate_copy(slot).start()

    def from_direct():
        cross().wait_recv()
        for i, r in enumerate([row] + sides):
            fan(i, r).start()

    def from_chain():
        share(0, row).wait_recv()
        for i, r in enumerate(sides):
            share(i, r).start()

    for d in range(n_groups - 2, n_groups):
        pl.when(jnp.logical_and(at_first, lower))(functools.partial(onward, d, group + d))
    pl.when(upper)(from_chain)
    pl.when(direct_in)(from_direct)
    for k in range(n_groups):
        for j in range(1, GROUP):
            handover(k, j)
    pl.when(jnp.logical_and(lower, at_last))(from_chain)
    for r in sides:
        copy(b_buf.at[r], b_buf.at[r], side_send.at[0], b_recv.at[r], at(r=r)).wait_recv()
    def half_arrived(i):
        slot = jnp.bitwise_xor(half, 2 * i)
        copy(b_buf.at[slot], b_buf.at[slot], fan_send.at[0], b_recv.at[slot], at(r=half, c=beside)).wait_recv()

    def b_side(h):
        return jnp.transpose(jnp.concatenate([b_buf[2 * x + h] for x in range(n_x)], axis=0))

    deep = 2 * GROUP * height
    a_part = 2 * GROUP * 2

    def contract(k, t, b_rows):
        g = jnp.bitwise_xor(group, k)
        rows = a_buf[pl.ds(pl.multiple_of(g * 2 * GROUP, 2 * GROUP), 2 * GROUP)].reshape(deep, LANES)
        integral[t] = jnp.dot(rows, b_rows, preferred_element_type=jnp.float32)
        start = pl.multiple_of(t * n_a + g * a_part, a_part)
        for c in range(width):
            lines = integral[t, pl.ds(c, a_part, stride=width), :]
            high = lines.astype(jnp.bfloat16)
            low = (lines - high.astype(jnp.float32)).astype(jnp.bfloat16)
            parts[pl.ds(start, a_part), c * span:(c + 1) * span] = high
            parts[pl.ds(pl.multiple_of(2 * n_a + start, a_part), a_part), c * span:(c + 1) * span] = low

    b_near = b_side(here)
    for k in range(n_groups):
        for p in range(GROUP):
            slot = (jnp.bitwise_xor(group, k) * GROUP + p) * 2 + 1 - core
            block(slot, mate_send.at[0], mate).wait_recv()
        contract(k, 0, b_near)
    pl.when(direct_in)(lambda: half_arrived(0))
    for i in range(1, n_x):
        half_arrived(i)
    b_far = b_side(1 - here)
    for k in range(n_groups):
        contract(k, 1, b_far)

    def give_sum(i):
        return copy(sums.at[others[i]], inbox.at[pair], r_send.at[i], r_recv.at[pair], at(p=others[i]))

    both = lax.dot_general(wide[...], parts[...], (((1,), (1,)), ((), ())), preferred_element_type=jnp.float32)
    for p in range(n_pairs):
        sums[p] = both[p * tall:(p + 1) * tall, 0:2 * n_a] + both[p * tall:(p + 1) * tall, 2 * n_a:4 * n_a]
    for i in range(len(others)):
        give_sum(i).start()
    total = sums[pair]
    for p in others:
        copy(sums.at[p], inbox.at[p], r_send.at[0], r_recv.at[p], at(p=p)).wait_recv()
        total = total + inbox[p]
    for s in range(slab):
        kept = jnp.where(label == symmetry[s], total[s * n_b:(s + 1) * n_b], 0.0)
        mine, far = kept[:, 0:n_a], kept[:, n_a:2 * n_a]
        even, odd = jnp.where(upper, far, mine), jnp.where(upper, mine, far)
        for x in range(n_x):
            out_ref[s, 4 * x:4 * x + 2, :] = even[2 * x:2 * x + 2]
            out_ref[s, 4 * x + 2:4 * x + 4, :] = odd[2 * x:2 * x + 2]

    for g in range(n_groups):
        slot = column(g, place)
        for j in range(GROUP - 1):
            near_copy(g, slot, j).wait_send()
        pl.when(jnp.logical_or(jnp.logical_and(g > group, passes_left), jnp.logical_and(g < group, has_right)))(
            functools.partial(lambda g: chain(g, left, g).wait_send(), g)
        )
    pl.when(has_left)(lambda: chain(group, left, n_groups).wait_send())
    pl.when(leap)(lambda: chain(group, left, n_groups + 2).wait_send())
    pl.when(has_right)(lambda: chain(group, right, n_groups + 1).wait_send())
    for c in range(n_cols // 2):
        mate_copy(2 * c + core).wait_send()
    for i, r in enumerate(sides):
        side(i, r).wait_send()
    pl.when(direct_in)(lambda: fan(0, row).wait_send())
    for i, r in enumerate(sides):
        share(i, r).wait_send()
    pl.when(direct_out)(lambda: cross().wait_send())
    pl.when(low_edge)(lambda: over(col, 0).wait_send())
    pl.when(low_edge)(lambda: over(col, 1).wait_send())
    pl.when(jnp.logical_and(upper, at_first))(lambda: over(col, 1).wait_send())
    for i in range(len(others)):
        give_weights(i).wait_send()
        give_sum(i).wait_send()


def body(factors, amplitudes, virt_irreps, win_irreps, occ_irreps, pair_list):
    n_rows, n_cols, n_pairs = (lax.axis_size(name) for name in ("row", "col", "pair"))
    slab, width = amplitudes.shape[0], amplitudes.shape[1]
    per_device = factors.shape[1]
    n_a = per_device * n_cols
    n_x = n_rows // 2
    n_b = n_x * per_device
    span = n_b * width
    n_groups = n_cols // 2 // GROUP
    height = per_device * width
    hbm = pl.BlockSpec(memory_space=pltpu.HBM)
    dma = pltpu.SemaphoreType.DMA
    out = pl.pallas_call(
        functools.partial(kernel, (n_rows, n_cols, n_pairs, slab)),
        out_shape=jax.ShapeDtypeStruct((slab, n_rows * per_device, n_a), jnp.float32),
        in_specs=[hbm] * 6,
        out_specs=pl.BlockSpec(memory_space=pltpu.VMEM),
        scratch_shapes=[
            pltpu.VMEM((per_device, width, factors.shape[0]), factors.dtype),
            pltpu.VMEM(amplitudes.shape, amplitudes.dtype),
            pltpu.SMEM(virt_irreps.shape, jnp.int32),
            pltpu.SMEM(win_irreps.shape, jnp.int32),
            pltpu.SMEM(occ_irreps.shape, jnp.int32),
            pltpu.SMEM(pair_list.shape[::-1], jnp.int32),
            dma((6,)),
            pltpu.VMEM((n_cols, height, LANES), jnp.bfloat16),
            pltpu.VMEM((n_rows, height, LANES), jnp.bfloat16),
            pltpu.VMEM((height, LANES), jnp.bfloat16),
            pltpu.VMEM((n_pairs, slab * width, width), jnp.bfloat16),
            pltpu.VMEM((n_pairs * slab * n_b, width * span), jnp.bfloat16),
            pltpu.VMEM((2, 2 * GROUP * height, span), jnp.float32),
            pltpu.VMEM((4 * n_a, width * span), jnp.bfloat16),
            pltpu.VMEM((n_pairs, slab * n_b, 2 * n_a), jnp.float32),
            pltpu.VMEM((n_pairs, slab * n_b, 2 * n_a), jnp.float32),
            dma((n_groups * (GROUP - 1),)), dma((n_cols // 2,)), dma((n_groups + 3,)), dma((n_cols,)),
            dma((n_x - 1,)), dma, dma((n_x,)), dma, dma((n_rows,)),
            dma((n_pairs,)), dma((n_pairs,)), dma((n_pairs,)), dma((n_pairs,)), dma((2,)),
            pltpu.SemaphoreType.REGULAR((2,)),
        ],
        compiler_params=pltpu.CompilerParams(
            collective_id=0, has_side_effects=True, vmem_limit_bytes=56 * 1024 * 1024
        ),
        name="ladder",
    )(jnp.transpose(factors, (1, 2, 0)), amplitudes, virt_irreps, win_irreps, occ_irreps, pair_list.T)
    return jnp.transpose(out.reshape(slab, n_rows, per_device, n_a), (0, 3, 1, 2))


def solution(mesh):
    in_specs = (P("pair", ("row", "col"), None), P("pair", None, None), P(), P(), P(), P())
    out_specs = P("pair", "row", None, "col")
    return jax.shard_map(body, mesh=mesh, in_specs=in_specs, out_specs=out_specs, check_vma=False)
```
